32 devices in a mesh: groups: 2 (over x), row: 16 (over z, y, core).
Axes of the slice: x: 2, y: 2, z: 4, core: 2. Of those that a mesh axis runs over, the one named last changes fastest.
Arguments:
- queries: bfloat16 [32, 5, 64, 768], P(('groups', 'row')), parts along dimension 0, may hold values from -20 to 20
- keys: bfloat16 [32, 5, 64, 768], P(('groups', 'row')), parts along dimension 0, may hold values from -20 to 20
- values: bfloat16 [32, 5, 64, 768], P(('groups', 'row')), parts along dimension 0, may hold values from -6 to 6
- outputs: bfloat16 [32, 5, 64, 768], P(('groups', 'row')), parts along dimension 0, may hold values from -6 to 6
- grad_out: bfloat16 [32, 5, 64, 1536], P(('groups', 'row')), parts along dimension 0, may hold values from -6 to 6
- w_out: bfloat16 [768, 1536], replicated, may hold values from -0.21875 to 0.21875
- bounds: int32 [32, 2], P('groups'), parts along dimension 0, may hold values from 0 to 15, as said below
Outputs:
- grad_queries: bfloat16 [32, 5, 64, 768], P(('groups', 'row')), parts along dimension 0
- grad_keys: bfloat16 [32, 5, 64, 768], P(('groups', 'row')), parts along dimension 0
- grad_values: bfloat16 [32, 5, 64, 768], P(('groups', 'row')), parts along dimension 0
- grad_w_out: float32 [1536, 1536], P(('groups', 'row')), parts along dimension 0
The draws below stay inside these ranges and needn't reach their ends.
There are 2 independent parts, one for each index of `groups`. The reference program is written for one: setup_inputs(seed, part) draws one part's arguments, and reference() takes and returns one part's arrays. A program takes and returns all parts, laid end to end along the dimension named above; an argument that names none is the same for every part. Nothing has to cross between parts.
Inputs may be any that keep to these rules, and one draw needn't show every extreme that they name: Images are packed one below another on the canvas, each covering whole tile rows; bounds[r, 0] <= r <= bounds[r, 1], and all tile rows of one image carry the same pair.
All inputs are finite; a program needn't handle non-finite values.
Results may differ from the reference program's by a relative error of at most 0.0058.
Values may be sent and summed in bfloat16 or wider, within the bound.
No kernel may reach another device: no remote copies, remote signals or barrier semaphores. Data moves between devices by JAX's collectives and lax.ppermute only.
A program may use at most 192 MiB of HBM per device.

```python
import jax
import jax.numpy as jnp
from jax import lax

D = 1536
HEADS = 12
HEAD = 64
TILE = 64
REACH = 3
TC = 5
TILE_ROWS = 16
HD = 768


def base_field(key, seed_mix):
    full_shape = (TILE_ROWS, TC, TILE, HEADS * HEAD)
    return jnp.clip(jax.random.normal(jax.random.fold_in(key, seed_mix), full_shape, jnp.float32), -4.0, 4.0)


def draw_queries(key, part):
    field = base_field(key, 11)
    return field.astype(jnp.bfloat16)


def draw_keys(key, part):
    field = base_field(key, 12)
    return field.astype(jnp.bfloat16)


def draw_bounds(key, part):
    image_starts = jax.random.randint(jax.random.fold_in(key, 31), (TILE_ROWS,), 0, 6) == 0
    image_starts = image_starts.at[0].set(True)
    row_index = jnp.arange(TILE_ROWS, dtype=jnp.int32)
    first_rows = lax.cummax(jnp.where(image_starts, row_index, 0), axis=0)
    start_marks = jnp.where(image_starts, row_index, TILE_ROWS).astype(jnp.int32)
    following = jnp.concatenate([start_marks[1:], jnp.array([TILE_ROWS], jnp.int32)])
    bottom = lax.cummin(following, axis=0, reverse=True) - 1
    return jnp.stack([first_rows, bottom], axis=1).astype(jnp.int32)


def spiked(values, own_key, source, target, shards_of, factor):
    owner, partner = [(jnp.arange(values.shape[axis_at]) // (values.shape[axis_at] // shards_of)).reshape([-1 if axis == axis_at else 1 for axis in range(values.ndim)]) for axis_at in (source, target)]
    chosen = jax.random.permutation(own_key, shards_of)[partner]
    strong = (owner == chosen) | (owner == (partner + shards_of // 2) % shards_of)
    return jnp.where(strong, factor * values, values)


def steps_of(key, dims, pieces, low, largest):
    factor_of, own = 1.0, jax.random.fold_in(key, 6)
    for axis_at, shards_of in pieces:
        steps = jnp.exp(jax.random.uniform(jax.random.fold_in(own, axis_at), (shards_of,), jnp.float32, low / len(pieces), largest / len(pieces)))
        factor_of = factor_of * jnp.repeat(steps, dims[axis_at] // shards_of).reshape([-1 if axis == axis_at else 1 for axis in range(len(dims))])
    return factor_of


def scatter_about(stream_key, shape, deviation, most, pieces=(), kind=jnp.bfloat16):
    values = jax.random.normal(stream_key, shape, jnp.float32) * deviation
    if len(pieces) > 0:
        values = steps_of(stream_key, shape, pieces, -0.22, 0.18) * values
    return jnp.clip(values, min=-most, max=most).astype(kind)


def bell_draw_with(key, shape, width, reach, shards, heavy, kind=jnp.bfloat16):
    result = width * jax.random.normal(key, shape, jnp.float32)
    if shards:
        result = result * steps_of(key, shape, shards, -0.22, 0.18)
    return jnp.clip(spiked(result, jax.random.fold_in(key, 3), *heavy), -reach, reach).astype(kind)


def setup_inputs(seed: int = 0, part: int = 0) -> dict:
    key_list = jax.random.split(jax.random.key(seed), 8)
    part_splits = jax.random.split(jax.random.fold_in(key_list[7], part), 8)
    queries = draw_queries(jax.random.fold_in(jax.random.fold_in(key_list[7], part), 71), part)
    keys = draw_keys(jax.random.fold_in(jax.random.fold_in(key_list[7], part), 71), part)
    values = scatter_about(part_splits[2], (TILE_ROWS, TC, TILE, HD), 1.0, 6.0, ((0, 16),))
    outputs = bell_draw_with(part_splits[3], (TILE_ROWS, TC, TILE, HD), 1.0, 6.0, ((0, 16),), (0, 3, 16, 2.0))
    grad_out = scatter_about(part_splits[4], (TILE_ROWS, TC, TILE, D), 1.0, 6.0, ((0, 16),))
    w_out = scatter_about(key_list[5], (HD, D), HD ** -0.5, 0.21875)
    bounds = draw_bounds(jax.random.fold_in(jax.random.fold_in(key_list[7], part), 71), part)
    return dict(queries=queries, keys=keys, values=values, outputs=outputs, grad_out=grad_out, w_out=w_out, bounds=bounds)


SCALE = 0.125
NEGATIVE = -1.0e30


def window_mask(centre, bounds, col_count, tile_len):
    window_rows = 2 * REACH + 1
    window_idx = jnp.arange(window_rows * col_count * tile_len, dtype=jnp.int32)
    other_row = centre - REACH + window_idx // (col_count * tile_len)
    other_col = (window_idx // tile_len) % col_count
    own_col = jnp.arange(col_count * tile_len, dtype=jnp.int32) // tile_len
    limits = lax.dynamic_index_in_dim(bounds, centre, 0, keepdims=False)
    row_ok = (other_row >= limits[0]) & (other_row <= limits[1])
    col_ok = jnp.abs(own_col[:, None] - other_col[None, :]) <= REACH
    return row_ok[None, :] & col_ok


def reference(queries, keys, values, outputs, grad_out, w_out, bounds):
    all_rows, col_count, tile_len, feature_count = queries.shape
    window_rows = 2 * REACH + 1
    flat_grad = grad_out.reshape(-1, grad_out.shape[3])
    grad_attn = jnp.dot(flat_grad, w_out.T, preferred_element_type=jnp.float32).astype(jnp.bfloat16)
    grad_attn = grad_attn.reshape(all_rows, col_count, tile_len, feature_count)
    widened = lax.optimization_barrier(grad_attn).astype(jnp.float32)
    grad_dot = jnp.sum((widened * outputs.astype(jnp.float32)).reshape(all_rows, col_count, tile_len, HEADS, HEAD), axis=4)
    padding = ((REACH, REACH), (0, 0), (0, 0), (0, 0))
    keys_padded = jnp.pad(keys, padding).astype(jnp.float32)
    values_padded = jnp.pad(values, padding).astype(jnp.float32)

    def step(totals, centre):
        allowed = window_mask(centre, bounds, col_count, tile_len)
        key_heads = lax.dynamic_slice_in_dim(keys_padded, centre, window_rows, 0).reshape(-1, HEADS, HEAD)
        value_heads = lax.dynamic_slice_in_dim(values_padded, centre, window_rows, 0).reshape(-1, HEADS, HEAD)
        query_heads = lax.dynamic_index_in_dim(queries, centre, 0, keepdims=False).reshape(-1, HEADS, HEAD).astype(jnp.float32)
        grad_heads = lax.dynamic_index_in_dim(widened, centre, 0, keepdims=False).reshape(-1, HEADS, HEAD)
        dot_here = lax.dynamic_index_in_dim(grad_dot, centre, 0, keepdims=False).reshape(-1, HEADS)
        scores = SCALE * jnp.einsum("qhe,khe->hqk", query_heads, key_heads)
        scores = jnp.where(allowed[None], scores, NEGATIVE)
        row_peak = jnp.max(scores, axis=2, keepdims=True)
        log_total = row_peak + jnp.log(jnp.sum(jnp.exp(scores - row_peak), axis=2, keepdims=True))
        softmax_out = jnp.exp(scores - log_total)
        grad_probs = jnp.einsum("qhe,khe->hqk", grad_heads, value_heads)
        grad_scores = softmax_out * (grad_probs - jnp.transpose(dot_here)[:, :, None])
        grad_scores = lax.optimization_barrier(grad_scores.astype(jnp.bfloat16)).astype(jnp.float32)
        weights = lax.optimization_barrier(softmax_out.astype(jnp.bfloat16)).astype(jnp.float32)
        grad_q = SCALE * jnp.einsum("hqk,khe->qhe", grad_scores, key_heads)
        grad_q = grad_q.reshape(-1, feature_count).astype(jnp.bfloat16)
        part_k = jnp.einsum("hqk,qhe->khe", grad_scores, query_heads)
        part_v = jnp.einsum("hqk,qhe->khe", weights, grad_heads)
        update = jnp.stack([part_k, part_v]).reshape(2, window_rows, col_count, tile_len, feature_count)
        current = lax.dynamic_slice_in_dim(totals, centre, window_rows, 1)
        totals = lax.dynamic_update_slice_in_dim(totals, current + update, centre, 1)
        return totals, grad_q

    start_totals = jnp.zeros((2, all_rows + 2 * REACH, col_count, tile_len, feature_count), jnp.float32)
    totals, grad_rows = lax.scan(step, start_totals, jnp.arange(all_rows, dtype=jnp.int32))
    grad_queries = grad_rows.reshape(all_rows, col_count, tile_len, feature_count)
    grad_keys = (SCALE * totals[0, REACH:REACH + all_rows]).astype(jnp.bfloat16)
    grad_values = totals[1, REACH:REACH + all_rows].astype(jnp.bfloat16)
    grad_w_out = jnp.dot(outputs.reshape(-1, feature_count).T, flat_grad, preferred_element_type=jnp.float32)
    return (grad_queries, grad_keys, grad_values, grad_w_out)
```

```python
import functools
import math

import jax
import jax.numpy as jnp
from jax import lax
from jax.experimental import pallas as pl
from jax.experimental.pallas import tpu as pltpu
from jax.sharding import PartitionSpec as P

HEAD = 64
REACH = 3
SCALE = 0.125
NEGATIVE = -1e30
GROUP = 4
LANES = 128
CHUNK = 256
WINDOW = 8

VMEM_SPEC = pl.BlockSpec(memory_space=pltpu.VMEM)
SMEM_SPEC = pl.BlockSpec(memory_space=pltpu.SMEM)
ANY_SPEC = pl.BlockSpec(memory_space=pl.ANY)
PARAMS = pltpu.CompilerParams(vmem_limit_bytes=56 * 1024 * 1024)


def lanes_below(shape):
    return lax.broadcasted_iota(jnp.int32, shape, len(shape) - 1) < HEAD


def pair_slab(left, right, head):
    columns = slice(head // 2 * LANES, (head // 2 + 1) * LANES)
    a, b = left[:, columns], right[:, columns]
    if head % 2:
        a = pltpu.roll(a, HEAD, 1)
    else:
        b = pltpu.roll(b, HEAD, 1)
    return jnp.where(lanes_below(a.shape), a, b)


def send_pieces(pieces, outs, sem, me):
    copies = []
    for target in range(GROUP):
        for slot in range(GROUP):
            copy = pltpu.make_async_copy(pieces.at[target], outs[slot], sem.at[target])
            copies.append((jnp.bitwise_xor(me, slot) == target, copy))
    for cond, copy in copies:
        pl.when(cond)(copy.start)
    for cond, copy in copies:
        pl.when(cond)(copy.wait)


def pack_kv_kernel(heads, me_ref, k_ref, v_ref, *rest):
    outs, (pieces, sem) = rest[:GROUP], rest[GROUP:]
    per = heads // GROUP
    for target in range(GROUP):
        for head in range(per):
            pieces[target, head] = pair_slab(k_ref, v_ref, target * per + head)
    send_pieces(pieces, outs, sem, me_ref[0])


def pack_qd_kernel(heads, me_ref, q_ref, grad_ref, w_ref, o_ref, *rest):
    outs, (pieces, sem, attn) = rest[:GROUP], rest[GROUP:]
    per = heads // GROUP
    tokens = q_ref.shape[0]
    lanes_up = -(-tokens // LANES) * LANES
    grad_attn = lax.dot_general(
        grad_ref[...], w_ref[...], (((1,), (1,)), ((), ())), preferred_element_type=jnp.float32
    ).astype(jnp.bfloat16)
    attn[...] = grad_attn
    product = grad_attn.astype(jnp.float32) * o_ref[...].astype(jnp.float32)
    lane = lax.broadcasted_iota(jnp.int32, (tokens, LANES), 1)
    for target in range(GROUP):
        columns = jnp.zeros((tokens, LANES), jnp.float32)
        for head in range(per):
            full = target * per + head
            pieces[target, head * tokens : (head + 1) * tokens] = pair_slab(q_ref, attn, full)
            dot = jnp.sum(product[:, full * HEAD : (full + 1) * HEAD], axis=1, keepdims=True)
            high = dot.astype(jnp.bfloat16).astype(jnp.float32)
            columns = jnp.where(lane == 2 * head, high, columns)
            columns = jnp.where(lane == 2 * head + 1, dot - high, columns)
        rows = jnp.transpose(columns)[:16]
        rows = jnp.concatenate([rows, jnp.zeros((16, lanes_up - tokens), jnp.float32)], axis=1)
        rows = rows.astype(jnp.bfloat16)
        for block in range(lanes_up // LANES):
            start = per * tokens + 16 * block
            pieces[target, start : start + 16] = rows[:, block * LANES : (block + 1) * LANES]
    send_pieces(pieces, outs, sem, me_ref[0])


def halo_kernel(me_ref, *refs):
    received, (up_ref, down_ref) = refs[:GROUP], refs[GROUP:]
    for slot in range(GROUP):
        row = jnp.bitwise_xor(me_ref[0], slot)

        @pl.when(row >= GROUP - REACH)
        def _():
            up_ref[row - GROUP + REACH] = received[slot][...]

        @pl.when(row < REACH)
        def _():
            down_ref[row] = received[slot][...]


def attention_kernel(per, cols, scalars, *refs):
    kv_refs = refs[:GROUP]
    above_ref, below_ref = refs[GROUP : GROUP + 2]
    qd_refs = refs[GROUP + 2 : 2 * GROUP + 2]
    outs = refs[2 * GROUP + 2 :]
    to_above, to_below, own_ref, dq_ref = outs[:4]
    k_buf, v_buf, q_buf, d_buf, qz_buf, dz_buf, delta_buf, s_all, dp_all, wds_all, zq_buf, acc, dq_buf, dqn_buf = outs[4:]
    head = pl.program_id(0)
    me, first_row = scalars[0], scalars[1]
    tokens = above_ref.shape[2]
    half = tokens // 2
    tile = tokens // cols
    rows_all = GROUP + 2 * REACH
    factor = SCALE * math.log2(math.e)
    bf16 = jnp.bfloat16
    zero = jnp.zeros((), bf16)

    lane = lax.broadcasted_iota(jnp.int32, (tokens, LANES), 1)
    low_half = lane < HEAD
    col_of = lax.broadcasted_iota(jnp.int32, (tokens, LANES), 0) // tile
    col_hot = lane == HEAD + 16 + col_of
    q_col_bias = (lane >= HEAD + 16) & (lane < HEAD + 16 + cols) & (jnp.abs(lane - (HEAD + 16) - col_of) > REACH)

    lows, highs = [], []
    for row in range(GROUP):
        here = first_row + row
        base = first_row - REACH
        lows.append(jnp.maximum(scalars[2 + 2 * row], here - REACH) - base)
        highs.append(jnp.minimum(scalars[3 + 2 * row], here + REACH) - base + 1)

    @pl.when(head == 0)
    def _():
        for slot in range(GROUP):
            row = jnp.bitwise_xor(me, slot)
            blocks = -(-tokens // LANES)
            lines = jnp.concatenate([qd_refs[slot][per * tokens + 16 * b : per * tokens + 16 * (b + 1)] for b in range(blocks)], axis=1)
            lines = jnp.concatenate([lines.astype(jnp.float32), jnp.zeros((LANES - 16, blocks * LANES), jnp.float32)], axis=0)
            delta_buf[row] = jnp.transpose(lines)[:tokens].astype(bf16)

    v_const = jnp.where((lane == 2 * head) | (lane == 2 * head + 1), -1.0, 0.0).astype(bf16)

    def put_kv(j, slab):
        where_j = pl.ds(pl.multiple_of(j * tokens, tokens), tokens)
        k_buf[where_j] = jnp.where(low_half, slab, jnp.where(col_hot | (lane == HEAD + j), 1.0, 0.0).astype(bf16))
        v_buf[where_j] = jnp.where(low_half, v_const, slab)

    for slot in range(GROUP):
        row = jnp.bitwise_xor(me, slot)
        put_kv(row + REACH, kv_refs[slot][head])
        qd = qd_refs[slot][pl.ds(pl.multiple_of(head * tokens, tokens), tokens)]
        low, high = lows[0], highs[0]
        for other in range(1, GROUP):
            low = jnp.where(row == other, lows[other], low)
            high = jnp.where(row == other, highs[other], high)
        at = lane - HEAD
        bias = q_col_bias | ((at >= 0) & (at < rows_all) & ((at < low) | (at >= high)))
        place = pl.ds(pl.multiple_of(row * tokens, tokens), tokens)
        q_buf[place] = jnp.where(low_half, qd, jnp.where(bias, NEGATIVE, 0.0).astype(bf16))
        d_buf[place] = jnp.where(low_half, delta_buf[row], qd)
        qz_buf[place] = jnp.where(low_half, qd, zero)
        dz_buf[place] = jnp.where(low_half, zero, qd)
    for row in range(REACH):
        put_kv(row, above_ref[row, head])
        put_kv(GROUP + REACH + row, below_ref[row, head])
    for c in range(GROUP * tokens // CHUNK):
        zq_buf[c, :CHUNK] = dz_buf[c * CHUNK:(c + 1) * CHUNK]
        zq_buf[c, CHUNK:] = qz_buf[c * CHUNK:(c + 1) * CHUNK]
    acc[...] = jnp.zeros_like(acc)
    nt = (((1,), (1,)), ((), ()))

    wide = WINDOW * tokens
    chunks = GROUP * tokens // CHUNK
    block = tokens

    for chunk in range(chunks):
        slot = chunk % 2
        s_buf, dp_buf, wds_buf = s_all.at[slot], dp_all.at[slot], wds_all.at[slot]
        first = min(chunk * CHUNK // tokens, rows_all - WINDOW)
        place = slice(chunk * CHUNK, (chunk + 1) * CHUNK)
        span = slice(first * tokens, first * tokens + wide)
        query = q_buf[place]
        grad = d_buf[place]
        s_buf[...] = lax.dot_general(k_buf[span], query, nt, preferred_element_type=jnp.float32)
        peak = jnp.full((8, CHUNK), NEGATIVE, jnp.float32)
        for at in range(0, wide, block):
            peak = jnp.maximum(peak, jnp.max(s_buf[at:at+block].reshape(block // 8, 8, CHUNK), axis=0))
        peak = jnp.max(peak, axis=0, keepdims=True)
        dp_buf[...] = lax.dot_general(v_buf[span], grad, nt, preferred_element_type=jnp.float32)
        total = jnp.zeros((8, CHUNK), jnp.float32)
        for at in range(0, wide, block):
            p = jnp.exp2((s_buf[at:at+block] - peak) * factor)
            s_buf[at:at+block] = p
            total = total + jnp.sum(p.reshape(block // 8, 8, CHUNK), axis=0)
        inverse = 1.0 / jnp.sum(total, axis=0, keepdims=True)
        for at in range(0, wide, block):
            p = s_buf[at:at+block] * inverse
            wds_buf[at:at+block, :CHUNK] = p.astype(bf16)
            wds_buf[at:at+block, CHUNK:] = (p * dp_buf[at:at+block]).astype(bf16)
        acc[span] += jnp.dot(wds_buf[...], zq_buf[chunk], preferred_element_type=jnp.float32)
        dq_buf[chunk] = lax.dot_general(k_buf[span], wds_buf[:, CHUNK:], (((0,), (0,)), ((), ())), preferred_element_type=jnp.float32)
    for chunk in range(chunks):
        dqn_buf[chunk * CHUNK:(chunk + 1) * CHUNK] = jnp.transpose(dq_buf[chunk])

    for row in range(REACH):
        to_above[row, head] = acc[row * tokens:(row + 1) * tokens].astype(bf16)
        to_below[row, head] = acc[(GROUP + REACH + row) * tokens:(GROUP + REACH + row + 1) * tokens].astype(bf16)
    for row in range(GROUP):
        own_ref[row, head] = acc[(REACH + row) * tokens:(REACH + row + 1) * tokens]
        dq = (SCALE * dqn_buf[row * tokens : (row + 1) * tokens]).astype(bf16)
        dq_ref[row, head] = jnp.where(low_half[:half], dq[:half], pltpu.roll(dq[half:], HEAD, 1))


def sum_kernel(per, me_ref, own_ref, above_ref, below_ref, *rest):
    outs, (pieces, sem) = rest[:GROUP], rest[GROUP:]
    for row in range(GROUP):
        for slab in range(per):
            value = own_ref[row, slab]
            if row < REACH:
                value = value + above_ref[row, slab].astype(jnp.float32)
            if row >= GROUP - REACH:
                value = value + below_ref[row - GROUP + REACH, slab].astype(jnp.float32)
            value = jnp.where(lanes_below(value.shape), value * SCALE, value)
            pieces[row, slab] = value.astype(jnp.bfloat16)
    send_pieces(pieces, outs, sem, me_ref[0])


def unpack_kernel(per, me_ref, *refs):
    dq_refs, kv_refs = refs[:GROUP], refs[GROUP : 2 * GROUP]
    q_out, k_out, v_out, dq_all, kv_all, sem = refs[2 * GROUP :]
    me = me_ref[0]
    half = dq_refs[0].shape[1]
    copies = []
    for slot in range(GROUP):
        source = jnp.bitwise_xor(me, slot)
        copies.append(pltpu.make_async_copy(dq_refs[slot], dq_all.at[source], sem.at[0, slot]))
        copies.append(pltpu.make_async_copy(kv_refs[slot], kv_all.at[source], sem.at[1, slot]))
    for copy in copies:
        copy.start()
    for copy in copies:
        copy.wait()
    for pair in range(GROUP * per // 2):
        (ga, ha), (gb, hb) = [divmod(2 * pair + step, per) for step in range(2)]
        columns = slice(pair * LANES, (pair + 1) * LANES)
        a, b = dq_all[ga, ha], dq_all[gb, hb]
        below = lanes_below(a.shape)
        q_out[:half, columns] = jnp.where(below, a, pltpu.roll(b, HEAD, 1))
        q_out[half:, columns] = jnp.where(below, pltpu.roll(a, HEAD, 1), b)
        a, b = kv_all[ga, ha], kv_all[gb, hb]
        below = lanes_below(a.shape)
        k_out[:, columns] = jnp.where(below, a, pltpu.roll(b, HEAD, 1))
        v_out[:, columns] = jnp.where(below, pltpu.roll(a, HEAD, 1), b)


def body(queries, keys, values, outputs, grad_out, w_out, bounds):
    own_rows, cols, tile, features = queries.shape
    tokens = own_rows * cols * tile
    half = tokens // 2
    heads = features // HEAD
    per = heads // GROUP
    count = lax.axis_size("row")
    assert own_rows == 1 and count % GROUP == 0 and heads % GROUP == 0
    bf16 = jnp.bfloat16
    position = lax.axis_index("row")
    me = (position % GROUP).astype(jnp.int32)
    first_row = position - me
    me_arr = me.reshape(1)
    q2, k2, v2, o2 = [x.reshape(tokens, features) for x in (queries, keys, values, outputs)]
    g2 = grad_out.reshape(tokens, -1)

    def exchange(pieces):
        result = [pieces[0]]
        for slot in range(1, GROUP):
            result.append(
                lax.ppermute(pieces[slot], "row", [(i, i ^ slot) for i in range(count)])
            )
        return result

    def shift(value, step):
        pairs = [(i, i + step) for i in range(count) if 0 <= i + step < count]
        return lax.ppermute(value, "row", pairs)

    def spread(rows):
        return [
            lax.dynamic_index_in_dim(rows, jnp.bitwise_xor(me, slot), 0, keepdims=False)
            for slot in range(GROUP)
        ]

    piece = (per, tokens, LANES)
    kv = pl.pallas_call(
        functools.partial(pack_kv_kernel, heads),
        out_shape=[jax.ShapeDtypeStruct(piece, bf16)] * GROUP,
        in_specs=[SMEM_SPEC, VMEM_SPEC, VMEM_SPEC],
        out_specs=[ANY_SPEC] * GROUP,
        scratch_shapes=[pltpu.VMEM((GROUP,) + piece, bf16), pltpu.SemaphoreType.DMA((GROUP,))],
        compiler_params=PARAMS,
        name="pack_kv",
    )(me_arr, k2, v2)
    kv = exchange(kv)

    qd_rows = per * tokens + 16 * (-(-tokens // LANES))
    qd = pl.pallas_call(
        functools.partial(pack_qd_kernel, heads),
        out_shape=[jax.ShapeDtypeStruct((qd_rows, LANES), bf16)] * GROUP,
        in_specs=[SMEM_SPEC] + [VMEM_SPEC] * 4,
        out_specs=[ANY_SPEC] * GROUP,
        scratch_shapes=[
            pltpu.VMEM((GROUP, qd_rows, LANES), bf16),
            pltpu.SemaphoreType.DMA((GROUP,)),
            pltpu.VMEM((tokens, features), bf16),
        ],
        compiler_params=PARAMS,
        name="pack_qd",
    )(me_arr, q2, g2, w_out, o2)
    qd = exchange(qd)

    window = (REACH,) + piece
    up, down = pl.pallas_call(
        halo_kernel,
        out_shape=[jax.ShapeDtypeStruct(window, bf16)] * 2,
        in_specs=[SMEM_SPEC] + [VMEM_SPEC] * GROUP,
        out_specs=[VMEM_SPEC] * 2,
        compiler_params=PARAMS,
        name="halo",
    )(me_arr, *kv)
    above = shift(up, GROUP)
    below = shift(down, -GROUP)

    limits = lax.dynamic_slice_in_dim(bounds, first_row, GROUP, 0).reshape(-1)
    scalars = jnp.concatenate([me_arr, first_row.reshape(1), limits])
    rows_all = GROUP + 2 * REACH
    chunks = GROUP * tokens // CHUNK
    results = pl.pallas_call(
        functools.partial(attention_kernel, per, cols),
        grid=(per,),
        out_shape=[
            jax.ShapeDtypeStruct(window, bf16),
            jax.ShapeDtypeStruct(window, bf16),
            jax.ShapeDtypeStruct((GROUP,) + piece, jnp.float32),
            jax.ShapeDtypeStruct((GROUP, per, half, LANES), bf16),
        ],
        in_specs=[SMEM_SPEC] + [VMEM_SPEC] * (2 * GROUP + 2),
        out_specs=[VMEM_SPEC] * 4,
        scratch_shapes=[pltpu.VMEM((rows_all * tokens, LANES), bf16)] * 2
        + [pltpu.VMEM((GROUP * tokens, LANES), bf16)] * 4
        + [
            pltpu.VMEM((GROUP, tokens, LANES), bf16),
            pltpu.VMEM((2, WINDOW * tokens, CHUNK), jnp.float32),
            pltpu.VMEM((2, WINDOW * tokens, CHUNK), jnp.float32),
            pltpu.VMEM((2, WINDOW * tokens, 2 * CHUNK), bf16),
            pltpu.VMEM((chunks, 2 * CHUNK, LANES), bf16),
            pltpu.VMEM((rows_all * tokens, LANES), jnp.float32),
            pltpu.VMEM((chunks, LANES, CHUNK), jnp.float32),
            pltpu.VMEM((GROUP * tokens, LANES), jnp.float32),
        ],
        compiler_params=PARAMS,
        name="attention",
    )(scalars, *kv, above, below, *qd)
    to_above, to_below, own, dq = results
    dq = exchange(spread(dq))
    from_above = shift(to_below, GROUP)
    from_below = shift(to_above, -GROUP)

    dkv = pl.pallas_call(
        functools.partial(sum_kernel, per),
        out_shape=[jax.ShapeDtypeStruct(piece, bf16)] * GROUP,
        in_specs=[SMEM_SPEC] + [VMEM_SPEC] * 3,
        out_specs=[ANY_SPEC] * GROUP,
        scratch_shapes=[pltpu.VMEM((GROUP,) + piece, bf16), pltpu.SemaphoreType.DMA((GROUP,))],
        compiler_params=PARAMS,
        name="sum",
    )(me_arr, own, from_above, from_below)
    dkv = exchange(dkv)

    grads = pl.pallas_call(
        functools.partial(unpack_kernel, per),
        out_shape=[jax.ShapeDtypeStruct((tokens, features), bf16)] * 3,
        in_specs=[SMEM_SPEC] + [ANY_SPEC] * (2 * GROUP),
        out_specs=[VMEM_SPEC] * 3,
        scratch_shapes=[
            pltpu.VMEM((GROUP, per, half, LANES), bf16),
            pltpu.VMEM((GROUP,) + piece, bf16),
            pltpu.SemaphoreType.DMA((2, GROUP)),
        ],
        compiler_params=PARAMS,
        name="unpack",
    )(me_arr, *dq, *dkv)
    grads = [x.reshape(queries.shape) for x in grads]

    grad_w_out = lax.psum_scatter(
        lax.dot_general(o2, g2, (((0,), (0,)), ((), ())), preferred_element_type=jnp.float32),
        "row",
        scatter_dimension=0,
        tiled=True,
    )
    return (*grads, grad_w_out)


def solution(mesh):
    placed = P(("groups", "row"), None, None, None)
    return jax.shard_map(
        body,
        mesh=mesh,
        in_specs=(placed, placed, placed, placed, placed, P(), P("groups", None)),
        out_specs=(placed, placed, placed, P(("groups", "row"), None)),
        check_vma=False,
    )
```

```python
import functools
import math

import jax
import jax.numpy as jnp
from jax import lax
from jax.experimental import pallas as pl
from jax.experimental.pallas import tpu as pltpu
from jax.sharding import PartitionSpec as P

HEAD = 64
REACH = 3
SCALE = 0.125
NEGATIVE = -1e30
GROUP = 4
LANES = 128
CHUNK = 256
WINDOW = 8

VMEM_SPEC = pl.BlockSpec(memory_space=pltpu.VMEM)
SMEM_SPEC = pl.BlockSpec(memory_space=pltpu.SMEM)
ANY_SPEC = pl.BlockSpec(memory_space=pl.ANY)
PARAMS = pltpu.CompilerParams(vmem_limit_bytes=56 * 1024 * 1024)


MICROS = {
    "pack_kv": 2.5,
    "pack_qd": 11,
    "last": 2,
    "fold": 2,
    "halo": 2.5,
    "attention": 14,
    "sum": 2.5,
    "unpack": 3,
}


def kernel_call(*args, micros, **options):
    cost = pl.CostEstimate(flops=int(micros * 1.1e9), bytes_accessed=0, transcendentals=0)
    return pl.pallas_call(*args, cost_estimate=cost, **options)


def lanes_below(shape):
    return lax.broadcasted_iota(jnp.int32, shape, len(shape) - 1) < HEAD


def pair_slab(left, right, head):
    columns = slice(head // 2 * LANES, (head // 2 + 1) * LANES)
    a, b = left[:, columns], right[:, columns]
    if head % 2:
        a = pltpu.roll(a, HEAD, 1)
    else:
        b = pltpu.roll(b, HEAD, 1)
    return jnp.where(lanes_below(a.shape), a, b)


def send_pieces(pieces, outs, sem, me):
    copies = []
    for target in range(GROUP):
        for slot in range(GROUP):
            copy = pltpu.make_async_copy(pieces.at[target], outs[slot], sem.at[target])
            copies.append((jnp.bitwise_xor(me, slot) == target, copy))
    for cond, copy in copies:
        pl.when(cond)(copy.start)
    for cond, copy in copies:
        pl.when(cond)(copy.wait)


def pack_kv_kernel(heads, me_ref, k_ref, v_ref, *rest):
    outs, (pieces, sem) = rest[:GROUP], rest[GROUP:]
    per = heads // GROUP
    for target in range(GROUP):
        for head in range(per):
            pieces[target, head] = pair_slab(k_ref, v_ref, target * per + head)
    send_pieces(pieces, outs, sem, me_ref[0])


def pack_qd_kernel(heads, count, me_ref, q_ref, grad_ref, w_ref, o_ref, *rest):
    outs, rest = rest[:GROUP], rest[GROUP:]
    if count:
        weight_part(count, me_ref[1], o_ref, grad_ref, *rest[:2], rest[-1])
        rest = rest[2:-1]
    pieces, sem, attn = rest
    per = heads // GROUP
    tokens = q_ref.shape[0]
    lanes_up = -(-tokens // LANES) * LANES
    grad_attn = lax.dot_general(
        grad_ref[...], w_ref[...], (((1,), (1,)), ((), ())), preferred_element_type=jnp.float32
    ).astype(jnp.bfloat16)
    attn[...] = grad_attn
    product = grad_attn.astype(jnp.float32) * o_ref[...].astype(jnp.float32)
    lane = lax.broadcasted_iota(jnp.int32, (tokens, LANES), 1)
    for target in range(GROUP):
        columns = jnp.zeros((tokens, LANES), jnp.float32)
        for head in range(per):
            full = target * per + head
            pieces[target, head * tokens : (head + 1) * tokens] = pair_slab(q_ref, attn, full)
            dot = jnp.sum(product[:, full * HEAD : (full + 1) * HEAD], axis=1, keepdims=True)
            high = dot.astype(jnp.bfloat16).astype(jnp.float32)
            columns = jnp.where(lane == 2 * head, high, columns)
            columns = jnp.where(lane == 2 * head + 1, dot - high, columns)
        rows = jnp.transpose(columns)[:16]
        rows = jnp.concatenate([rows, jnp.zeros((16, lanes_up - tokens), jnp.float32)], axis=1)
        rows = rows.astype(jnp.bfloat16)
        for block in range(lanes_up // LANES):
            start = per * tokens + 16 * block
            pieces[target, start : start + 16] = rows[:, block * LANES : (block + 1) * LANES]
    send_pieces(pieces, outs, sem, me_ref[0])


def halo_kernel(me_ref, *refs):
    received, (up_ref, down_ref) = refs[:GROUP], refs[GROUP:]
    for slot in range(GROUP):
        row = jnp.bitwise_xor(me_ref[0], slot)

        @pl.when(row >= GROUP - REACH)
        def _():
            up_ref[:, row - GROUP + REACH] = received[slot][...]

        @pl.when(row < REACH)
        def _():
            down_ref[:, row] = received[slot][...]


def attention_kernel(per, cols, first_head, scalars, *refs):
    kv_refs = refs[:GROUP]
    above_ref, below_ref = refs[GROUP : GROUP + 2]
    qd_refs = refs[GROUP + 2 : 2 * GROUP + 2]
    delta_refs = refs[2 * GROUP + 2 : 3 * GROUP + 2]
    to_above, to_below, own_ref, dq_ref = refs[3 * GROUP + 2 : 3 * GROUP + 6]
    k_buf, v_buf, q_buf, d_buf, s_buf, dp_buf, wds_buf, zq_buf, acc, dq_buf = refs[3 * GROUP + 6 :]
    me, first_row = scalars[0], scalars[1]
    head = first_head + pl.program_id(0)
    tokens = above_ref.shape[2]
    half = tokens // 2
    tile = tokens // cols
    rows_all = GROUP + 2 * REACH
    chunks = GROUP * tokens // CHUNK
    wide = WINDOW * tokens
    factor = SCALE * math.log2(math.e)
    bf16, f32 = jnp.bfloat16, jnp.float32
    zero = jnp.zeros((), bf16)

    lane = lax.broadcasted_iota(jnp.int32, (tokens, LANES), 1)
    low_half = lane < HEAD
    at = lane - HEAD
    col_of = lax.broadcasted_iota(jnp.int32, (tokens, LANES), 0) // tile
    col_hot = at == 16 + col_of
    col_bias = (at >= 16) & (at < 16 + cols) & (jnp.abs(at - 16 - col_of) > REACH)
    v_const = jnp.where((lane == 2 * head) | (lane == 2 * head + 1), -1.0, 0.0).astype(bf16)

    def put_kv(j, slab):
        place = pl.ds(pl.multiple_of(j * tokens, tokens), tokens)
        hot = jnp.where(col_hot | (at == j), 1.0, 0.0).astype(bf16)
        k_buf[place] = jnp.where(low_half, slab, hot)
        v_buf[place] = jnp.where(low_half, v_const, slab)

    for slot in range(GROUP):
        row = jnp.bitwise_xor(me, slot)
        put_kv(row + REACH, kv_refs[slot][0])
        here = first_row + row
        base = first_row - REACH
        low = jnp.maximum(scalars[2 + 2 * row], here - REACH) - base
        high = jnp.minimum(scalars[3 + 2 * row], here + REACH) - base
        bias = col_bias | ((at >= 0) & (at < rows_all) & ((at < low) | (at > high)))
        qd = qd_refs[slot][...]
        place = pl.ds(pl.multiple_of(row * tokens, tokens), tokens)
        q_buf[place] = jnp.where(low_half, qd, jnp.where(bias, NEGATIVE, 0.0).astype(bf16))
        blocks = -(-tokens // LANES)
        lines = [delta_refs[slot][16 * b : 16 * (b + 1)] for b in range(blocks)]
        lines = jnp.concatenate(lines, axis=1).astype(f32)
        lines = jnp.concatenate(
            [lines, jnp.zeros((LANES - 16, blocks * LANES), f32)], axis=0
        )
        d_buf[place] = jnp.where(low_half, jnp.transpose(lines)[:tokens].astype(bf16), qd)
    for row in range(REACH):
        put_kv(row, above_ref[0, row])
        put_kv(GROUP + REACH + row, below_ref[0, row])
    chunk_low = lax.broadcasted_iota(jnp.int32, (CHUNK, LANES), 1) < HEAD
    for chunk in range(chunks):
        place = slice(chunk * CHUNK, (chunk + 1) * CHUNK)
        zq_buf[chunk, :CHUNK] = jnp.where(chunk_low, zero, d_buf[place])
        zq_buf[chunk, CHUNK:] = jnp.where(chunk_low, q_buf[place], zero)
    acc[...] = jnp.zeros_like(acc)

    nt = (((1,), (1,)), ((), ()))
    tn = (((0,), (0,)), ((), ()))
    starts = [min(c * CHUNK // tokens, rows_all - WINDOW) for c in range(chunks)]
    spans = [slice(f * tokens, f * tokens + wide) for f in starts]
    places = [slice(c * CHUNK, (c + 1) * CHUNK) for c in range(chunks)]

    def products(c):
        s_buf[c % 2] = lax.dot_general(
            k_buf[spans[c]], q_buf[places[c]], nt, preferred_element_type=f32
        )
        dp_buf[c % 2] = lax.dot_general(
            v_buf[spans[c]], d_buf[places[c]], nt, preferred_element_type=f32
        )

    products(0)
    for c in range(chunks):
        if c + 1 < chunks:
            products(c + 1)
        s_ref, dp_ref, wds_ref = s_buf.at[c % 2], dp_buf.at[c % 2], wds_buf.at[c % 2]
        peak = jnp.full((8, CHUNK), NEGATIVE, f32)
        for first in range(0, wide, tokens):
            part = s_ref[first : first + tokens].reshape(tokens // 8, 8, CHUNK)
            peak = jnp.maximum(peak, jnp.max(part, axis=0))
        peak = jnp.max(peak, axis=0, keepdims=True)
        total = jnp.zeros((8, CHUNK), f32)
        for first in range(0, wide, tokens):
            p = jnp.exp2((s_ref[first : first + tokens] - peak) * factor)
            s_ref[first : first + tokens] = p
            total = total + jnp.sum(p.reshape(tokens // 8, 8, CHUNK), axis=0)
        inverse = 1.0 / jnp.sum(total, axis=0, keepdims=True)
        for first in range(0, wide, tokens):
            p = s_ref[first : first + tokens] * inverse
            wds_ref[first : first + tokens, :CHUNK] = p.astype(bf16)
            wds_ref[first : first + tokens, CHUNK:] = (
                p * dp_ref[first : first + tokens]
            ).astype(bf16)
        acc[spans[c]] += jnp.dot(wds_ref[...], zq_buf[c], preferred_element_type=f32)
        dq_buf[c] = lax.dot_general(
            k_buf[spans[c]], wds_ref[:, CHUNK:], tn, preferred_element_type=f32
        )

    grad_q = jnp.concatenate([jnp.transpose(dq_buf[c]) for c in range(chunks)], axis=0)
    grad_q = (SCALE * grad_q).astype(bf16)
    for row in range(REACH):
        last = GROUP + REACH + row
        to_above[0, row] = acc[row * tokens : (row + 1) * tokens].astype(bf16)
        to_below[0, row] = acc[last * tokens : (last + 1) * tokens].astype(bf16)
    for row in range(GROUP):
        own_ref[0, row] = acc[(REACH + row) * tokens : (REACH + row + 1) * tokens]
        dq = grad_q[row * tokens : (row + 1) * tokens]
        dq_ref[0, row] = jnp.where(low_half[:half], dq[:half], pltpu.roll(dq[half:], HEAD, 1))


def sum_kernel(me_ref, own_ref, above_ref, below_ref, dq_ref, *rest):
    outs, (pieces, sem) = rest[:GROUP], rest[GROUP:]
    tokens, half = own_ref.shape[2], dq_ref.shape[2]
    for head in range(own_ref.shape[0]):
        for row in range(GROUP):
            value = own_ref[head, row]
            if row < REACH:
                value = value + above_ref[head, row].astype(jnp.float32)
            if row >= GROUP - REACH:
                value = value + below_ref[head, row - GROUP + REACH].astype(jnp.float32)
            value = jnp.where(lanes_below(value.shape), value * SCALE, value)
            first = head * (tokens + half)
            pieces[row, first : first + tokens] = value.astype(jnp.bfloat16)
            pieces[row, first + tokens : first + tokens + half] = dq_ref[head, row]
    send_pieces(pieces, outs, sem, me_ref[0])


def unpack_kernel(split, me_ref, *refs):
    sets = len(split)
    parts, (q_out, k_out, v_out) = refs[: sets * GROUP], refs[sets * GROUP : sets * GROUP + 3]
    buffers, sem = refs[sets * GROUP + 3 : -1], refs[-1]
    me = me_ref[0]
    tokens = k_out.shape[0]
    half = tokens // 2
    per = sum(split)
    copies = []
    for at in range(sets):
        for slot in range(GROUP):
            source = jnp.bitwise_xor(me, slot)
            copies.append(
                pltpu.make_async_copy(
                    parts[at * GROUP + slot], buffers[at].at[source], sem.at[at, slot]
                )
            )
    for copy in copies:
        copy.start()
    for copy in copies:
        copy.wait()
    where = [(at, index) for at, number in enumerate(split) for index in range(number)]

    def piece(head):
        group, local = divmod(head, per)
        at, index = where[local]
        first = index * (tokens + half)
        return (
            buffers[at][group, first : first + tokens],
            buffers[at][group, first + tokens : first + tokens + half],
        )

    for pair in range(GROUP * per // 2):
        columns = slice(pair * LANES, (pair + 1) * LANES)
        (a, qa), (b, qb) = piece(2 * pair), piece(2 * pair + 1)
        below = lanes_below(qa.shape)
        q_out[:half, columns] = jnp.where(below, qa, pltpu.roll(qb, HEAD, 1))
        q_out[half:, columns] = jnp.where(below, pltpu.roll(qa, HEAD, 1), qb)
        below = lanes_below(a.shape)
        k_out[:, columns] = jnp.where(below, a, pltpu.roll(b, HEAD, 1))
        v_out[:, columns] = jnp.where(below, pltpu.roll(a, HEAD, 1), b)


def weight_part(count, at, o_ref, grad_ref, send_ref, left_ref, permuted):
    block = o_ref.shape[1] // count
    bits = count.bit_length() - 1
    order = [sum((i >> b & 1) << (bits - 1 - b) for b in range(bits)) for i in range(count)]
    for at_block, owner in enumerate(order):
        columns = slice(owner * block, (owner + 1) * block)
        permuted[:, at_block * block : (at_block + 1) * block] = o_ref[:, columns]
    rows = send_ref.shape[0]
    mine = at % 2
    send_ref[...] = outer(
        permuted[:, pl.ds(pl.multiple_of((1 - mine) * rows, rows), rows)], grad_ref[...]
    ).astype(send_ref.dtype)
    left_ref[...] = permuted[:, pl.ds(pl.multiple_of(mine * rows, rows), rows)]


def outer(left, right):
    return lax.dot_general(
        left, right, (((0,), (0,)), ((), ())), preferred_element_type=jnp.float32
    )


def second_kernel(at_ref, left_ref, grad_ref, received_ref, keep_ref, send_ref):
    rows = keep_ref.shape[0]
    mine = at_ref[0] // 2 % 2
    first, second = left_ref[:, :rows], left_ref[:, rows:]
    for other, out in ((1, send_ref), (0, keep_ref)):
        part = jnp.bitwise_xor(mine, other)
        place = pl.ds(pl.multiple_of(part * rows, rows), rows)
        left = jnp.where(part == 0, first, second)
        value = outer(left, grad_ref[...]) + received_ref[place].astype(jnp.float32)
        out[...] = value.astype(out.dtype)


def fold_kernel(bit, at_ref, kept_ref, received_ref, keep_ref, send_ref):
    rows = keep_ref.shape[0]
    mine = at_ref[0] // (1 << bit) % 2
    for other, out in ((1, send_ref), (0, keep_ref)):
        place = pl.ds(pl.multiple_of(jnp.bitwise_xor(mine, other) * rows, rows), rows)
        out[...] = (kept_ref[place] + received_ref[place].astype(jnp.float32)).astype(out.dtype)


def last_kernel(kept_ref, received_ref, out_ref):
    out_ref[...] = kept_ref[...] + received_ref[...].astype(jnp.float32)


def body(queries, keys, values, outputs, grad_out, w_out, bounds):
    own_rows, cols, tile, features = queries.shape
    tokens = own_rows * cols * tile
    half = tokens // 2
    heads = features // HEAD
    per = heads // GROUP
    count = lax.axis_size("row")
    assert own_rows == 1 and count % GROUP == 0 and heads % GROUP == 0
    bf16 = jnp.bfloat16
    position = lax.axis_index("row")
    me = (position % GROUP).astype(jnp.int32)
    first_row = position - me
    me_arr = me.reshape(1)
    q2, k2, v2, o2 = [x.reshape(tokens, features) for x in (queries, keys, values, outputs)]
    g2 = grad_out.reshape(tokens, -1)

    def exchange(pieces):
        result = [pieces[0]]
        for slot in range(1, GROUP):
            result.append(
                lax.ppermute(pieces[slot], "row", [(i, i ^ slot) for i in range(count)])
            )
        return result

    def shift(value, step):
        pairs = [(i, i + step) for i in range(count) if 0 <= i + step < count]
        return lax.ppermute(value, "row", pairs)

    def after(value, *others):
        return lax.optimization_barrier((value, *others))[0]

    piece = (per, tokens, LANES)
    kv = kernel_call(
        functools.partial(pack_kv_kernel, heads),
        out_shape=[jax.ShapeDtypeStruct(piece, bf16)] * GROUP,
        in_specs=[SMEM_SPEC, VMEM_SPEC, VMEM_SPEC],
        out_specs=[ANY_SPEC] * GROUP,
        scratch_shapes=[pltpu.VMEM((GROUP,) + piece, bf16), pltpu.SemaphoreType.DMA((GROUP,))],
        compiler_params=PARAMS,
        name="pack_kv",
            micros=MICROS["pack_kv"],
    )(me_arr, k2, v2)
    kv = exchange(kv)

    bits = count.bit_length() - 1
    halving = count == 1 << bits and features // count % 16 == 0
    shape = jax.ShapeDtypeStruct
    width = g2.shape[1]
    at_arr = position.astype(jnp.int32).reshape(1)

    def hop(sent, bit):
        return lax.ppermute(sent, "row", [(i, i ^ (1 << bit)) for i in range(count)])

    def halves(kernel, rows, bit, operands):
        return kernel_call(
            kernel,
            out_shape=[shape((rows, width), jnp.float32), shape((rows, width), bf16)],
            in_specs=[SMEM_SPEC] + [VMEM_SPEC] * (len(operands) - 1),
            out_specs=[VMEM_SPEC] * 2,
            compiler_params=PARAMS,
            name="fold",
            micros=MICROS["fold"],
        )(*operands)

    def fold(bit, kept, sent, other):
        operands = (after(at_arr, other), kept, hop(sent, bit))
        return halves(functools.partial(fold_kernel, bit + 1), kept.shape[0] // 2, bit, operands)

    qd_rows = per * tokens + 16 * (-(-tokens // LANES))
    rows = features // 2
    made = kernel_call(
        functools.partial(pack_qd_kernel, heads, count if halving else 0),
        out_shape=[shape((qd_rows, LANES), bf16)] * GROUP
        + [shape((rows, width), bf16), shape((tokens, rows), bf16)] * halving,
        in_specs=[SMEM_SPEC] + [VMEM_SPEC] * 4,
        out_specs=[ANY_SPEC] * GROUP + [VMEM_SPEC] * (2 * halving),
        scratch_shapes=[
            pltpu.VMEM((GROUP, qd_rows, LANES), bf16),
            pltpu.SemaphoreType.DMA((GROUP,)),
            pltpu.VMEM((tokens, features), bf16),
        ]
        + [pltpu.VMEM((tokens, features), bf16)] * halving,
        compiler_params=PARAMS,
        name="pack_qd",
        micros=MICROS["pack_qd"],
    )(after(jnp.concatenate([me_arr, at_arr]), kv[1]), q2, g2, w_out, o2)
    qd = made[:GROUP]
    if halving:
        sent, left = made[GROUP:]
    qd_sent = qd[1]
    qd = exchange(qd)

    groups = [number for number in (per - 1, 1) if number]
    window = (REACH, tokens, LANES)
    borders = kernel_call(
        halo_kernel,
        out_shape=[shape((per,) + window, bf16)] * 2,
        in_specs=[SMEM_SPEC] + [VMEM_SPEC] * GROUP,
        out_specs=[VMEM_SPEC] * 2,
        compiler_params=PARAMS,
        name="halo",
        micros=MICROS["halo"],
    )(after(me_arr, qd_sent), *kv)

    if halving:
        kept, sent = halves(
            second_kernel, features // 4, 0, (after(at_arr, borders[0]), left, g2, hop(after(sent, borders[0]), 0))
        )
    folds = 1
    limits = lax.dynamic_slice_in_dim(bounds, first_row, GROUP, 0).reshape(-1)
    scalars = jnp.concatenate([me_arr, first_row.reshape(1), limits])
    rows_all = GROUP + 2 * REACH
    chunks = GROUP * tokens // CHUNK
    delta_rows = qd_rows - per * tokens
    results = []
    head = 0
    ready = []
    above = shift(borders[0], GROUP)
    below = shift(borders[1], -GROUP)
    for number in groups:
        if halving:
            scalars = after(scalars, kept)
        here = lambda i: (i, 0, 0, 0)
        result = kernel_call(
            functools.partial(attention_kernel, per, cols, head),
            grid=(number,),
            out_shape=[
                shape((number,) + window, bf16),
                shape((number,) + window, bf16),
                shape((number, GROUP, tokens, LANES), jnp.float32),
                shape((number, GROUP, half, LANES), bf16),
            ],
            in_specs=[SMEM_SPEC]
            + [pl.BlockSpec((1, tokens, LANES), lambda i, head=head: (head + i, 0, 0))] * GROUP
            + [pl.BlockSpec((1,) + window, lambda i, head=head: (head + i, 0, 0, 0))] * 2
            + [pl.BlockSpec((tokens, LANES), lambda i, head=head: (head + i, 0))] * GROUP
            + [pl.BlockSpec((delta_rows, LANES), lambda i: (per * tokens // delta_rows, 0))]
            * GROUP,
            out_specs=[
                pl.BlockSpec((1,) + window, here),
                pl.BlockSpec((1,) + window, here),
                pl.BlockSpec((1, GROUP, tokens, LANES), here),
                pl.BlockSpec((1, GROUP, half, LANES), here),
            ],
            scratch_shapes=[pltpu.VMEM((rows_all * tokens, LANES), bf16)] * 2
            + [pltpu.VMEM((GROUP * tokens, LANES), bf16)] * 2
            + [
                pltpu.VMEM((2, WINDOW * tokens, CHUNK), jnp.float32),
                pltpu.VMEM((2, WINDOW * tokens, CHUNK), jnp.float32),
                pltpu.VMEM((2, WINDOW * tokens, 2 * CHUNK), bf16),
                pltpu.VMEM((chunks, 2 * CHUNK, LANES), bf16),
                pltpu.VMEM((rows_all * tokens, LANES), jnp.float32),
                pltpu.VMEM((chunks, LANES, CHUNK), jnp.float32),
            ],
            compiler_params=PARAMS,
            name="attention",
            micros=MICROS["attention"] * number,
        )(scalars, *kv, above, below, *qd, *qd)
        results.append(result)
        head += number
        if halving and folds < bits - 1:
            kept, sent = fold(folds, kept, sent, result[2])
            folds += 1

    if halving:
        while folds < bits - 1:
            kept, sent = fold(folds, kept, sent, results[-1][2])
            folds += 1
        ready = [kept]
    returned = []
    turn = after(me_arr, results[-1][2], *ready)
    for number, (to_above, to_below, own, dq) in zip(groups, results):
        size = (number * (tokens + half), LANES)
        pieces = kernel_call(
            sum_kernel,
            out_shape=[shape(size, bf16)] * GROUP,
            in_specs=[SMEM_SPEC] + [VMEM_SPEC] * 4,
            out_specs=[ANY_SPEC] * GROUP,
            scratch_shapes=[pltpu.VMEM((GROUP,) + size, bf16), pltpu.SemaphoreType.DMA((GROUP,))],
            compiler_params=PARAMS,
            name="sum",
            micros=MICROS["sum"],
        )(turn, own, shift(to_below, GROUP), shift(to_above, -GROUP), dq)
        returned += exchange(pieces)
        turn = after(me_arr, returned[3])

    if halving:
        grad_w_out = kernel_call(
            last_kernel,
            out_shape=shape(kept.shape, jnp.float32),
            in_specs=[VMEM_SPEC] * 2,
            out_specs=VMEM_SPEC,
            name="last",
            micros=MICROS["last"],
        )(after(kept, pieces[0]), hop(sent, bits - 1))
    else:
        grad_w_out = lax.psum_scatter(
            lax.dot_general(o2, g2, (((0,), (0,)), ((), ())), preferred_element_type=jnp.float32),
            "row",
            scatter_dimension=0,
            tiled=True,
        )

    grads = kernel_call(
        functools.partial(unpack_kernel, groups),
        out_shape=[shape((tokens, features), bf16)] * 3,
        in_specs=[SMEM_SPEC] + [ANY_SPEC] * (len(groups) * GROUP),
        out_specs=[VMEM_SPEC] * 3,
        scratch_shapes=[
            pltpu.VMEM((GROUP, number * (tokens + half), LANES), bf16) for number in groups
        ]
        + [pltpu.SemaphoreType.DMA((len(groups), GROUP))],
        compiler_params=PARAMS,
        name="unpack",
            micros=MICROS["unpack"],
    )(after(me_arr, grad_w_out), *returned)
    grads = [x.reshape(queries.shape) for x in grads]
    return (*grads, grad_w_out)


def solution(mesh):
    placed = P(("groups", "row"), None, None, None)
    return jax.shard_map(
        body,
        mesh=mesh,
        in_specs=(placed, placed, placed, placed, placed, P(), P("groups", None)),
        out_specs=(placed, placed, placed, P(("groups", "row"), None)),
        check_vma=False,
    )
```

```python
import functools
import math

import jax
import jax.numpy as jnp
from jax import lax
from jax.experimental import pallas as pl
from jax.experimental.pallas import tpu as pltpu
from jax.sharding import PartitionSpec as P

HEAD = 64
REACH = 3
SCALE = 0.125
NEGATIVE = -1e30
GROUP = 4
LANES = 128
CHUNK = 256
WINDOW = 8

VMEM_SPEC = pl.BlockSpec(memory_space=pltpu.VMEM)
SMEM_SPEC = pl.BlockSpec(memory_space=pltpu.SMEM)
ANY_SPEC = pl.BlockSpec(memory_space=pl.ANY)
PARAMS = pltpu.CompilerParams(vmem_limit_bytes=40 * 1024 * 1024)


MICROS = {
    "pack_kv": 2.5,
    "pack_qd": 11,
    "last": 2,
    "fold": 2,
    "halo": 2.5,
    "attention": 14,
    "sum": 2.5,
    "unpack": 3,
}


def kernel_call(*args, micros, **options):
    cost = pl.CostEstimate(flops=int(micros * 1.1e9), bytes_accessed=0, transcendentals=0)
    return pl.pallas_call(*args, cost_estimate=cost, **options)


def near(value):
    return pltpu.with_memory_space_constraint(value, pltpu.VMEM)


def lanes_below(shape):
    return lax.broadcasted_iota(jnp.int32, shape, len(shape) - 1) < HEAD


def pair_slab(left, right, head):
    columns = slice(head // 2 * LANES, (head // 2 + 1) * LANES)
    a, b = left[:, columns], right[:, columns]
    if head % 2:
        a = pltpu.roll(a, HEAD, 1)
    else:
        b = pltpu.roll(b, HEAD, 1)
    return jnp.where(lanes_below(a.shape), a, b)


def send_pieces(pieces, outs, sem, me):
    copies = []
    for target in range(GROUP):
        for slot in range(GROUP):
            copy = pltpu.make_async_copy(pieces.at[target], outs[slot], sem.at[target])
            copies.append((jnp.bitwise_xor(me, slot) == target, copy))
    for cond, copy in copies:
        pl.when(cond)(copy.start)
    for cond, copy in copies:
        pl.when(cond)(copy.wait)


def pack_kv_kernel(heads, me_ref, k_ref, v_ref, *rest):
    outs, (pieces, sem) = rest[:GROUP], rest[GROUP:]
    per = heads // GROUP
    for target in range(GROUP):
        for head in range(per):
            pieces[target, head] = pair_slab(k_ref, v_ref, target * per + head)
    send_pieces(pieces, outs, sem, me_ref[0])


def pack_qd_kernel(heads, count, me_ref, q_ref, grad_ref, w_ref, o_ref, *rest):
    outs, rest = rest[:GROUP], rest[GROUP:]
    if count:
        weight_part(count, me_ref[1], o_ref, grad_ref, *rest[:2], rest[-1])
        rest = rest[2:-1]
    pieces, sem, attn = rest
    per = heads // GROUP
    tokens = q_ref.shape[0]
    lanes_up = -(-tokens // LANES) * LANES
    grad_attn = lax.dot_general(
        grad_ref[...], w_ref[...], (((1,), (1,)), ((), ())), preferred_element_type=jnp.float32
    ).astype(jnp.bfloat16)
    attn[...] = grad_attn
    product = grad_attn.astype(jnp.float32) * o_ref[...].astype(jnp.float32)
    lane = lax.broadcasted_iota(jnp.int32, (tokens, LANES), 1)
    for target in range(GROUP):
        columns = jnp.zeros((tokens, LANES), jnp.float32)
        for head in range(per):
            full = target * per + head
            pieces[target, head * tokens : (head + 1) * tokens] = pair_slab(q_ref, attn, full)
            dot = jnp.sum(product[:, full * HEAD : (full + 1) * HEAD], axis=1, keepdims=True)
            high = dot.astype(jnp.bfloat16).astype(jnp.float32)
            columns = jnp.where(lane == 2 * head, high, columns)
            columns = jnp.where(lane == 2 * head + 1, dot - high, columns)
        rows = jnp.transpose(columns)[:16]
        rows = jnp.concatenate([rows, jnp.zeros((16, lanes_up - tokens), jnp.float32)], axis=1)
        rows = rows.astype(jnp.bfloat16)
        for block in range(lanes_up // LANES):
            start = per * tokens + 16 * block
            pieces[target, start : start + 16] = rows[:, block * LANES : (block + 1) * LANES]
    send_pieces(pieces, outs, sem, me_ref[0])


def halo_kernel(me_ref, *refs):
    received, (up_ref, down_ref) = refs[:GROUP], refs[GROUP:]
    for slot in range(GROUP):
        row = jnp.bitwise_xor(me_ref[0], slot)

        @pl.when(row >= GROUP - REACH)
        def _():
            up_ref[:, row - GROUP + REACH] = received[slot][...]

        @pl.when(row < REACH)
        def _():
            down_ref[:, row] = received[slot][...]


def attention_kernel(per, cols, first_head, scalars, *refs):
    kv_refs = refs[:GROUP]
    above_ref, below_ref = refs[GROUP : GROUP + 2]
    qd_refs = refs[GROUP + 2 : 2 * GROUP + 2]
    to_above, to_below, own_ref, dq_ref = refs[2 * GROUP + 2 : 2 * GROUP + 6]
    k_buf, v_buf, q_buf, d_buf, s_buf, dp_buf, wds_buf, zq_buf, acc, dq_buf = refs[2 * GROUP + 6 :]
    me, first_row = scalars[0], scalars[1]
    head = first_head + pl.program_id(0)
    tokens = above_ref.shape[2]
    half = tokens // 2
    tile = tokens // cols
    rows_all = GROUP + 2 * REACH
    chunks = GROUP * tokens // CHUNK
    wide = WINDOW * tokens
    factor = SCALE * math.log2(math.e)
    bf16, f32 = jnp.bfloat16, jnp.float32
    zero = jnp.zeros((), bf16)

    lane = lax.broadcasted_iota(jnp.int32, (tokens, LANES), 1)
    low_half = lane < HEAD
    at = lane - HEAD
    col_of = lax.broadcasted_iota(jnp.int32, (tokens, LANES), 0) // tile
    col_hot = at == 16 + col_of
    col_bias = (at >= 16) & (at < 16 + cols) & (jnp.abs(at - 16 - col_of) > REACH)
    v_const = jnp.where((lane == 2 * head) | (lane == 2 * head + 1), -1.0, 0.0).astype(bf16)

    def put_kv(j, slab):
        place = pl.ds(pl.multiple_of(j * tokens, tokens), tokens)
        hot = jnp.where(col_hot | (at == j), 1.0, 0.0).astype(bf16)
        k_buf[place] = jnp.where(low_half, slab, hot)
        v_buf[place] = jnp.where(low_half, v_const, slab)

    for slot in range(GROUP):
        row = jnp.bitwise_xor(me, slot)
        put_kv(row + REACH, kv_refs[slot][head])
        here = first_row + row
        base = first_row - REACH
        low = jnp.maximum(scalars[2 + 2 * row], here - REACH) - base
        high = jnp.minimum(scalars[3 + 2 * row], here + REACH) - base
        bias = col_bias | ((at >= 0) & (at < rows_all) & ((at < low) | (at > high)))
        qd = qd_refs[slot][pl.ds(pl.multiple_of(head * tokens, tokens), tokens)]
        place = pl.ds(pl.multiple_of(row * tokens, tokens), tokens)
        q_buf[place] = jnp.where(low_half, qd, jnp.where(bias, NEGATIVE, 0.0).astype(bf16))
        blocks = -(-tokens // LANES)
        ends = [per * tokens + 16 * b for b in range(blocks)]
        lines = [qd_refs[slot][end : end + 16] for end in ends]
        lines = jnp.concatenate(lines, axis=1).astype(f32)
        lines = jnp.concatenate(
            [lines, jnp.zeros((LANES - 16, blocks * LANES), f32)], axis=0
        )
        d_buf[place] = jnp.where(low_half, jnp.transpose(lines)[:tokens].astype(bf16), qd)
    for row in range(REACH):
        put_kv(row, above_ref[head, row])
        put_kv(GROUP + REACH + row, below_ref[head, row])
    chunk_low = lax.broadcasted_iota(jnp.int32, (CHUNK, LANES), 1) < HEAD
    for chunk in range(chunks):
        place = slice(chunk * CHUNK, (chunk + 1) * CHUNK)
        zq_buf[chunk, :CHUNK] = jnp.where(chunk_low, zero, d_buf[place])
        zq_buf[chunk, CHUNK:] = jnp.where(chunk_low, q_buf[place], zero)
    acc[...] = jnp.zeros_like(acc)

    nt = (((1,), (1,)), ((), ()))
    tn = (((0,), (0,)), ((), ()))
    starts = [min(c * CHUNK // tokens, rows_all - WINDOW) for c in range(chunks)]
    spans = [slice(f * tokens, f * tokens + wide) for f in starts]
    places = [slice(c * CHUNK, (c + 1) * CHUNK) for c in range(chunks)]

    def products(c):
        s_buf[c % 2] = lax.dot_general(
            k_buf[spans[c]], q_buf[places[c]], nt, preferred_element_type=f32
        )
        dp_buf[c % 2] = lax.dot_general(
            v_buf[spans[c]], d_buf[places[c]], nt, preferred_element_type=f32
        )

    products(0)
    for c in range(chunks):
        if c + 1 < chunks:
            products(c + 1)
        s_ref, dp_ref, wds_ref = s_buf.at[c % 2], dp_buf.at[c % 2], wds_buf.at[c % 2]
        peak = jnp.full((8, CHUNK), NEGATIVE, f32)
        for first in range(0, wide, tokens):
            part = s_ref[first : first + tokens].reshape(tokens // 8, 8, CHUNK)
            peak = jnp.maximum(peak, jnp.max(part, axis=0))
        peak = jnp.max(peak, axis=0, keepdims=True)
        total = jnp.zeros((8, CHUNK), f32)
        for first in range(0, wide, tokens):
            p = jnp.exp2((s_ref[first : first + tokens] - peak) * factor)
            s_ref[first : first + tokens] = p
            total = total + jnp.sum(p.reshape(tokens // 8, 8, CHUNK), axis=0)
        inverse = 1.0 / jnp.sum(total, axis=0, keepdims=True)
        for first in range(0, wide, tokens):
            p = s_ref[first : first + tokens] * inverse
            wds_ref[first : first + tokens, :CHUNK] = p.astype(bf16)
            wds_ref[first : first + tokens, CHUNK:] = (
                p * dp_ref[first : first + tokens]
            ).astype(bf16)
        acc[spans[c]] += jnp.dot(wds_ref[...], zq_buf[c], preferred_element_type=f32)
        dq_buf[c] = lax.dot_general(
            k_buf[spans[c]], wds_ref[:, CHUNK:], tn, preferred_element_type=f32
        )

    grad_q = jnp.concatenate([jnp.transpose(dq_buf[c]) for c in range(chunks)], axis=0)
    grad_q = (SCALE * grad_q).astype(bf16)
    for row in range(REACH):
        last = GROUP + REACH + row
        to_above[0, row] = acc[row * tokens : (row + 1) * tokens].astype(bf16)
        to_below[0, row] = acc[last * tokens : (last + 1) * tokens].astype(bf16)
    for row in range(GROUP):
        own_ref[0, row] = acc[(REACH + row) * tokens : (REACH + row + 1) * tokens]
        dq = grad_q[row * tokens : (row + 1) * tokens]
        dq_ref[0, row] = jnp.where(low_half[:half], dq[:half], pltpu.roll(dq[half:], HEAD, 1))


def sum_kernel(me_ref, own_ref, above_ref, below_ref, dq_ref, *rest):
    outs, (pieces, sem) = rest[:GROUP], rest[GROUP:]
    tokens, half = own_ref.shape[2], dq_ref.shape[2]
    for head in range(own_ref.shape[0]):
        for row in range(GROUP):
            value = own_ref[head, row]
            if row < REACH:
                value = value + above_ref[head, row].astype(jnp.float32)
            if row >= GROUP - REACH:
                value = value + below_ref[head, row - GROUP + REACH].astype(jnp.float32)
            value = jnp.where(lanes_below(value.shape), value * SCALE, value)
            first = head * (tokens + half)
            pieces[row, first : first + tokens] = value.astype(jnp.bfloat16)
            pieces[row, first + tokens : first + tokens + half] = dq_ref[head, row]
    send_pieces(pieces, outs, sem, me_ref[0])


def unpack_kernel(split, me_ref, *refs):
    sets = len(split)
    parts, (q_out, k_out, v_out) = refs[: sets * GROUP], refs[sets * GROUP : sets * GROUP + 3]
    buffers = refs[sets * GROUP + 3 :]
    me = me_ref[0]
    tokens = k_out.shape[0]
    half = tokens // 2
    per = sum(split)
    for at in range(sets):
        for slot in range(GROUP):
            buffers[at][jnp.bitwise_xor(me, slot)] = parts[at * GROUP + slot][...]
    where = [(at, index) for at, number in enumerate(split) for index in range(number)]

    def piece(head):
        group, local = divmod(head, per)
        at, index = where[local]
        first = index * (tokens + half)
        return (
            buffers[at][group, first : first + tokens],
            buffers[at][group, first + tokens : first + tokens + half],
        )

    for pair in range(GROUP * per // 2):
        columns = slice(pair * LANES, (pair + 1) * LANES)
        (a, qa), (b, qb) = piece(2 * pair), piece(2 * pair + 1)
        below = lanes_below(qa.shape)
        q_out[:half, columns] = jnp.where(below, qa, pltpu.roll(qb, HEAD, 1))
        q_out[half:, columns] = jnp.where(below, pltpu.roll(qa, HEAD, 1), qb)
        below = lanes_below(a.shape)
        k_out[:, columns] = jnp.where(below, a, pltpu.roll(b, HEAD, 1))
        v_out[:, columns] = jnp.where(below, pltpu.roll(a, HEAD, 1), b)


def weight_part(count, at, o_ref, grad_ref, send_ref, left_ref, permuted):
    block = o_ref.shape[1] // count
    bits = count.bit_length() - 1
    order = [sum((i >> b & 1) << (bits - 1 - b) for b in range(bits)) for i in range(count)]
    for at_block, owner in enumerate(order):
        columns = slice(owner * block, (owner + 1) * block)
        permuted[:, at_block * block : (at_block + 1) * block] = o_ref[:, columns]
    rows = send_ref.shape[0]
    mine = at % 2
    send_ref[...] = outer(
        permuted[:, pl.ds(pl.multiple_of((1 - mine) * rows, rows), rows)], grad_ref[...]
    ).astype(send_ref.dtype)
    left_ref[...] = permuted[:, pl.ds(pl.multiple_of(mine * rows, rows), rows)]


def outer(left, right):
    return lax.dot_general(
        left, right, (((0,), (0,)), ((), ())), preferred_element_type=jnp.float32
    )


def second_kernel(at_ref, left_ref, grad_ref, received_ref, keep_ref, send_ref):
    rows = keep_ref.shape[0]
    mine = at_ref[0] // 2 % 2
    first, second = left_ref[:, :rows], left_ref[:, rows:]
    for other, out in ((1, send_ref), (0, keep_ref)):
        part = jnp.bitwise_xor(mine, other)
        place = pl.ds(pl.multiple_of(part * rows, rows), rows)
        left = jnp.where(part == 0, first, second)
        value = outer(left, grad_ref[...]) + received_ref[place].astype(jnp.float32)
        out[...] = value.astype(out.dtype)


def fold_kernel(bit, at_ref, kept_ref, received_ref, keep_ref, send_ref):
    rows = keep_ref.shape[0]
    mine = at_ref[0] // (1 << bit) % 2
    for other, out in ((1, send_ref), (0, keep_ref)):
        place = pl.ds(pl.multiple_of(jnp.bitwise_xor(mine, other) * rows, rows), rows)
        out[...] = (kept_ref[place] + received_ref[place].astype(jnp.float32)).astype(out.dtype)


def last_kernel(kept_ref, received_ref, out_ref):
    out_ref[...] = kept_ref[...] + received_ref[...].astype(jnp.float32)


def body(queries, keys, values, outputs, grad_out, w_out, bounds):
    own_rows, cols, tile, features = queries.shape
    tokens = own_rows * cols * tile
    half = tokens // 2
    heads = features // HEAD
    per = heads // GROUP
    count = lax.axis_size("row")
    assert own_rows == 1 and count % GROUP == 0 and heads % GROUP == 0
    bf16 = jnp.bfloat16
    position = lax.axis_index("row")
    me = (position % GROUP).astype(jnp.int32)
    first_row = position - me
    me_arr = me.reshape(1)
    q2, k2, v2, o2 = [x.reshape(tokens, features) for x in (queries, keys, values, outputs)]
    g2 = grad_out.reshape(tokens, -1)

    def exchange(pieces):
        result = [pieces[0]]
        for slot in range(1, GROUP):
            pairs = [(i, i ^ slot) for i in range(count)]
            result.append(near(lax.ppermute(pieces[slot], "row", pairs)))
        return result

    def shift(value, step):
        pairs = [(i, i + step) for i in range(count) if 0 <= i + step < count]
        return near(lax.ppermute(value, "row", pairs))

    def after(value, *others):
        return lax.optimization_barrier((value, *others))[0]

    piece = (per, tokens, LANES)
    kv = kernel_call(
        functools.partial(pack_kv_kernel, heads),
        out_shape=[jax.ShapeDtypeStruct(piece, bf16)] * GROUP,
        in_specs=[SMEM_SPEC, VMEM_SPEC, VMEM_SPEC],
        out_specs=[ANY_SPEC] * GROUP,
        scratch_shapes=[pltpu.VMEM((GROUP,) + piece, bf16), pltpu.SemaphoreType.DMA((GROUP,))],
        compiler_params=PARAMS,
        name="pack_kv",
            micros=MICROS["pack_kv"],
    )(me_arr, k2, v2)
    kv = exchange(kv)

    bits = count.bit_length() - 1
    halving = count == 1 << bits and features // count % 16 == 0
    shape = jax.ShapeDtypeStruct
    width = g2.shape[1]
    at_arr = position.astype(jnp.int32).reshape(1)

    def hop(sent, bit):
        return near(lax.ppermute(sent, "row", [(i, i ^ (1 << bit)) for i in range(count)]))

    def halves(kernel, rows, bit, operands):
        return kernel_call(
            kernel,
            out_shape=[shape((rows, width), jnp.float32), shape((rows, width), bf16)],
            in_specs=[SMEM_SPEC] + [VMEM_SPEC] * (len(operands) - 1),
            out_specs=[VMEM_SPEC] * 2,
            compiler_params=PARAMS,
            name="fold",
            micros=MICROS["fold"],
        )(*operands)

    def fold(bit, kept, sent, other):
        operands = (after(at_arr, other), kept, hop(sent, bit))
        return halves(functools.partial(fold_kernel, bit + 1), kept.shape[0] // 2, bit, operands)

    qd_rows = per * tokens + 16 * (-(-tokens // LANES))
    rows = features // 2
    made = kernel_call(
        functools.partial(pack_qd_kernel, heads, count if halving else 0),
        out_shape=[shape((qd_rows, LANES), bf16)] * GROUP
        + [shape((rows, width), bf16), shape((tokens, rows), bf16)] * halving,
        in_specs=[SMEM_SPEC] + [VMEM_SPEC] * 4,
        out_specs=[ANY_SPEC] * GROUP + [VMEM_SPEC] * (2 * halving),
        scratch_shapes=[
            pltpu.VMEM((GROUP, qd_rows, LANES), bf16),
            pltpu.SemaphoreType.DMA((GROUP,)),
            pltpu.VMEM((tokens, features), bf16),
        ]
        + [pltpu.VMEM((tokens, features), bf16)] * halving,
        compiler_params=PARAMS,
        name="pack_qd",
        micros=MICROS["pack_qd"],
    )(after(jnp.concatenate([me_arr, at_arr]), kv[1]), q2, g2, w_out, o2)
    qd = made[:GROUP]
    if halving:
        sent, left = made[GROUP:]
    qd_sent = qd[1]
    qd = exchange(qd)

    groups = [number for number in (per - 1, 1) if number]
    window = (REACH, tokens, LANES)
    borders = kernel_call(
        halo_kernel,
        out_shape=[shape((per,) + window, bf16)] * 2,
        in_specs=[SMEM_SPEC] + [VMEM_SPEC] * GROUP,
        out_specs=[VMEM_SPEC] * 2,
        compiler_params=PARAMS,
        name="halo",
        micros=MICROS["halo"],
    )(after(me_arr, qd_sent), *kv)

    if halving:
        kept, sent = halves(
            second_kernel, features // 4, 0, (after(at_arr, borders[0]), left, g2, hop(after(sent, borders[0]), 0))
        )
    folds = 1
    limits = lax.dynamic_slice_in_dim(bounds, first_row, GROUP, 0).reshape(-1)
    scalars = jnp.concatenate([me_arr, first_row.reshape(1), limits])
    rows_all = GROUP + 2 * REACH
    chunks = GROUP * tokens // CHUNK
    results = []
    head = 0
    ready = []
    above = shift(borders[0], GROUP)
    below = shift(borders[1], -GROUP)
    for number in groups:
        if halving:
            scalars = after(scalars, kept)
        here = lambda i: (i, 0, 0, 0)
        result = kernel_call(
            functools.partial(attention_kernel, per, cols, head),
            grid=(number,),
            out_shape=[
                shape((number,) + window, bf16),
                shape((number,) + window, bf16),
                shape((number, GROUP, tokens, LANES), jnp.float32),
                shape((number, GROUP, half, LANES), bf16),
            ],
            in_specs=[SMEM_SPEC] + [VMEM_SPEC] * (2 * GROUP + 2),
            out_specs=[
                pl.BlockSpec((1,) + window, here),
                pl.BlockSpec((1,) + window, here),
                pl.BlockSpec((1, GROUP, tokens, LANES), here),
                pl.BlockSpec((1, GROUP, half, LANES), here),
            ],
            scratch_shapes=[pltpu.VMEM((rows_all * tokens, LANES), bf16)] * 2
            + [pltpu.VMEM((GROUP * tokens, LANES), bf16)] * 2
            + [
                pltpu.VMEM((2, WINDOW * tokens, CHUNK), jnp.float32),
                pltpu.VMEM((2, WINDOW * tokens, CHUNK), jnp.float32),
                pltpu.VMEM((2, WINDOW * tokens, 2 * CHUNK), bf16),
                pltpu.VMEM((chunks, 2 * CHUNK, LANES), bf16),
                pltpu.VMEM((rows_all * tokens, LANES), jnp.float32),
                pltpu.VMEM((chunks, LANES, CHUNK), jnp.float32),
            ],
            compiler_params=PARAMS,
            name="attention",
            micros=MICROS["attention"] * number,
        )(scalars, *kv, above, below, *qd)
        results.append(result)
        head += number
        if halving and folds < bits - 1:
            kept, sent = fold(folds, kept, sent, result[2])
            folds += 1

    if halving:
        while folds < bits - 1:
            kept, sent = fold(folds, kept, sent, results[-1][2])
            folds += 1
        ready = [kept]
    returned = []
    turn = after(me_arr, results[-1][2], *ready)
    for number, (to_above, to_below, own, dq) in zip(groups, results):
        size = (number * (tokens + half), LANES)
        pieces = kernel_call(
            sum_kernel,
            out_shape=[shape(size, bf16)] * GROUP,
            in_specs=[SMEM_SPEC] + [VMEM_SPEC] * 4,
            out_specs=[ANY_SPEC] * GROUP,
            scratch_shapes=[pltpu.VMEM((GROUP,) + size, bf16), pltpu.SemaphoreType.DMA((GROUP,))],
            compiler_params=PARAMS,
            name="sum",
            micros=MICROS["sum"],
        )(turn, own, shift(to_below, GROUP), shift(to_above, -GROUP), dq)
        returned += exchange(pieces)
        turn = after(me_arr, returned[3])

    if halving:
        grad_w_out = kernel_call(
            last_kernel,
            out_shape=shape(kept.shape, jnp.float32),
            in_specs=[VMEM_SPEC] * 2,
            out_specs=VMEM_SPEC,
            name="last",
            micros=MICROS["last"],
        )(after(kept, pieces[0]), hop(sent, bits - 1))
    else:
        grad_w_out = lax.psum_scatter(
            lax.dot_general(o2, g2, (((0,), (0,)), ((), ())), preferred_element_type=jnp.float32),
            "row",
            scatter_dimension=0,
            tiled=True,
        )

    grads = kernel_call(
        functools.partial(unpack_kernel, groups),
        out_shape=[shape((tokens, features), bf16)] * 3,
        in_specs=[SMEM_SPEC] + [VMEM_SPEC] * (len(groups) * GROUP),
        out_specs=[VMEM_SPEC] * 3,
        scratch_shapes=[
            pltpu.VMEM((GROUP, number * (tokens + half), LANES), bf16) for number in groups
        ],
        compiler_params=PARAMS,
        name="unpack",
            micros=MICROS["unpack"],
    )(after(me_arr, grad_w_out), *[near(x) for x in returned])
    grads = [x.reshape(queries.shape) for x in grads]
    return (*grads, grad_w_out)


def solution(mesh):
    placed = P(("groups", "row"), None, None, None)
    return jax.shard_map(
        body,
        mesh=mesh,
        in_specs=(placed, placed, placed, placed, placed, P(), P("groups", None)),
        out_specs=(placed, placed, placed, P(("groups", "row"), None)),
        check_vma=False,
    )
```

```python
import functools
import math

import jax
import jax.numpy as jnp
from jax import lax
from jax.experimental import pallas as pl
from jax.experimental.pallas import tpu as pltpu
from jax.sharding import PartitionSpec as P

HEAD = 64
REACH = 3
SCALE = 0.125
NEGATIVE = -1e30
GROUP = 4
LANES = 128
CHUNK = 256
WINDOW = 8

VMEM_SPEC = pl.BlockSpec(memory_space=pltpu.VMEM)
SMEM_SPEC = pl.BlockSpec(memory_space=pltpu.SMEM)
ANY_SPEC = pl.BlockSpec(memory_space=pl.ANY)
PARAMS = pltpu.CompilerParams(vmem_limit_bytes=28 * 1024 * 1024)


MICROS = {
    "pack_kv": 2.5,
    "pack_qd": 11,
    "last": 2,
    "fold": 2,
    "halo": 2.5,
    "attention": 14,
    "sum": 2.5,
    "unpack": 3,
}


def kernel_call(*args, micros, **options):
    cost = pl.CostEstimate(flops=int(micros * 1.1e9), bytes_accessed=0, transcendentals=0)
    return pl.pallas_call(*args, cost_estimate=cost, **options)


def near(value):
    return pltpu.with_memory_space_constraint(value, pltpu.VMEM)


def lanes_below(shape):
    return lax.broadcasted_iota(jnp.int32, shape, len(shape) - 1) < HEAD


def pair_slab(left, right, head):
    columns = slice(head // 2 * LANES, (head // 2 + 1) * LANES)
    a, b = left[:, columns], right[:, columns]
    if head % 2:
        a = pltpu.roll(a, HEAD, 1)
    else:
        b = pltpu.roll(b, HEAD, 1)
    return jnp.where(lanes_below(a.shape), a, b)


def send_pieces(pieces, outs, sem, me):
    copies = []
    for target in range(GROUP):
        for slot in range(GROUP):
            copy = pltpu.make_async_copy(pieces.at[target], outs[slot], sem.at[target])
            copies.append((jnp.bitwise_xor(me, slot) == target, copy))
    for cond, copy in copies:
        pl.when(cond)(copy.start)
    for cond, copy in copies:
        pl.when(cond)(copy.wait)


def pack_kv_kernel(heads, me_ref, k_ref, v_ref, *rest):
    outs, (pieces, sem) = rest[:GROUP], rest[GROUP:]
    per = heads // GROUP
    for target in range(GROUP):
        for head in range(per):
            pieces[target, head] = pair_slab(k_ref, v_ref, target * per + head)
    send_pieces(pieces, outs, sem, me_ref[0])


def pack_qd_kernel(heads, count, me_ref, q_ref, grad_ref, w_ref, o_ref, *rest):
    outs, rest = rest[:GROUP], rest[GROUP:]
    if count:
        weight_part(count, me_ref[1], o_ref, grad_ref, *rest[:2], rest[-1])
        rest = rest[2:-1]
    pieces, sem, attn = rest
    per = heads // GROUP
    tokens = q_ref.shape[0]
    lanes_up = -(-tokens // LANES) * LANES
    grad_attn = lax.dot_general(
        grad_ref[...], w_ref[...], (((1,), (1,)), ((), ())), preferred_element_type=jnp.float32
    ).astype(jnp.bfloat16)
    attn[...] = grad_attn
    product = grad_attn.astype(jnp.float32) * o_ref[...].astype(jnp.float32)
    lane = lax.broadcasted_iota(jnp.int32, (tokens, LANES), 1)
    for target in range(GROUP):
        columns = jnp.zeros((tokens, LANES), jnp.float32)
        for head in range(per):
            full = target * per + head
            pieces[target, head * tokens : (head + 1) * tokens] = pair_slab(q_ref, attn, full)
            dot = jnp.sum(product[:, full * HEAD : (full + 1) * HEAD], axis=1, keepdims=True)
            high = dot.astype(jnp.bfloat16).astype(jnp.float32)
            columns = jnp.where(lane == 2 * head, high, columns)
            columns = jnp.where(lane == 2 * head + 1, dot - high, columns)
        rows = jnp.transpose(columns)[:16]
        rows = jnp.concatenate([rows, jnp.zeros((16, lanes_up - tokens), jnp.float32)], axis=1)
        rows = rows.astype(jnp.bfloat16)
        for block in range(lanes_up // LANES):
            start = per * tokens + 16 * block
            pieces[target, start : start + 16] = rows[:, block * LANES : (block + 1) * LANES]
    send_pieces(pieces, outs, sem, me_ref[0])


def halo_kernel(me_ref, *refs):
    received, (up_ref, down_ref) = refs[:GROUP], refs[GROUP:]
    for slot in range(GROUP):
        row = jnp.bitwise_xor(me_ref[0], slot)

        @pl.when(row >= GROUP - REACH)
        def _():
            up_ref[:, row - GROUP + REACH] = received[slot][...]

        @pl.when(row < REACH)
        def _():
            down_ref[:, row] = received[slot][...]


def attention_kernel(per, cols, first_head, scalars, *refs):
    kv_refs = refs[:GROUP]
    above_ref, below_ref = refs[GROUP : GROUP + 2]
    qd_refs = refs[GROUP + 2 : 2 * GROUP + 2]
    to_above, to_below, own_ref, dq_ref = refs[2 * GROUP + 2 : 2 * GROUP + 6]
    k_buf, v_buf, q_buf, d_buf, s_buf, dp_buf, wds_buf, zq_buf, acc, dq_buf = refs[2 * GROUP + 6 :]
    me, first_row = scalars[0], scalars[1]
    head = first_head + pl.program_id(0)
    tokens = above_ref.shape[2]
    half = tokens // 2
    tile = tokens // cols
    rows_all = GROUP + 2 * REACH
    chunks = GROUP * tokens // CHUNK
    wide = WINDOW * tokens
    factor = SCALE * math.log2(math.e)
    bf16, f32 = jnp.bfloat16, jnp.float32
    zero = jnp.zeros((), bf16)

    lane = lax.broadcasted_iota(jnp.int32, (tokens, LANES), 1)
    low_half = lane < HEAD
    at = lane - HEAD
    col_of = lax.broadcasted_iota(jnp.int32, (tokens, LANES), 0) // tile
    col_hot = at == 16 + col_of
    col_bias = (at >= 16) & (at < 16 + cols) & (jnp.abs(at - 16 - col_of) > REACH)
    v_const = jnp.where((lane == 2 * head) | (lane == 2 * head + 1), -1.0, 0.0).astype(bf16)

    def put_kv(j, slab):
        place = pl.ds(pl.multiple_of(j * tokens, tokens), tokens)
        hot = jnp.where(col_hot | (at == j), 1.0, 0.0).astype(bf16)
        k_buf[place] = jnp.where(low_half, slab, hot)
        v_buf[place] = jnp.where(low_half, v_const, slab)

    for slot in range(GROUP):
        row = jnp.bitwise_xor(me, slot)
        put_kv(row + REACH, kv_refs[slot][head])
        here = first_row + row
        base = first_row - REACH
        low = jnp.maximum(scalars[2 + 2 * row], here - REACH) - base
        high = jnp.minimum(scalars[3 + 2 * row], here + REACH) - base
        bias = col_bias | ((at >= 0) & (at < rows_all) & ((at < low) | (at > high)))
        qd = qd_refs[slot][pl.ds(pl.multiple_of(head * tokens, tokens), tokens)]
        place = pl.ds(pl.multiple_of(row * tokens, tokens), tokens)
        q_buf[place] = jnp.where(low_half, qd, jnp.where(bias, NEGATIVE, 0.0).astype(bf16))
        blocks = -(-tokens // LANES)
        ends = [per * tokens + 16 * b for b in range(blocks)]
        lines = [qd_refs[slot][end : end + 16] for end in ends]
        lines = jnp.concatenate(lines, axis=1).astype(f32)
        lines = jnp.concatenate(
            [lines, jnp.zeros((LANES - 16, blocks * LANES), f32)], axis=0
        )
        d_buf[place] = jnp.where(low_half, jnp.transpose(lines)[:tokens].astype(bf16), qd)
    for row in range(REACH):
        put_kv(row, above_ref[head, row])
        put_kv(GROUP + REACH + row, below_ref[head, row])
    chunk_low = lax.broadcasted_iota(jnp.int32, (CHUNK, LANES), 1) < HEAD
    for chunk in range(chunks):
        place = slice(chunk * CHUNK, (chunk + 1) * CHUNK)
        zq_buf[chunk, :CHUNK] = jnp.where(chunk_low, zero, d_buf[place])
        zq_buf[chunk, CHUNK:] = jnp.where(chunk_low, q_buf[place], zero)
    acc[...] = jnp.zeros_like(acc)

    nt = (((1,), (1,)), ((), ()))
    tn = (((0,), (0,)), ((), ()))
    starts = [min(c * CHUNK // tokens, rows_all - WINDOW) for c in range(chunks)]
    spans = [slice(f * tokens, f * tokens + wide) for f in starts]
    places = [slice(c * CHUNK, (c + 1) * CHUNK) for c in range(chunks)]

    def products(c):
        s_buf[c % 2] = lax.dot_general(
            k_buf[spans[c]], q_buf[places[c]], nt, preferred_element_type=f32
        )
        dp_buf[c % 2] = lax.dot_general(
            v_buf[spans[c]], d_buf[places[c]], nt, preferred_element_type=f32
        )

    products(0)
    for c in range(chunks):
        if c + 1 < chunks:
            products(c + 1)
        s_ref, dp_ref, wds_ref = s_buf.at[c % 2], dp_buf.at[c % 2], wds_buf.at[c % 2]
        peak = jnp.full((8, CHUNK), NEGATIVE, f32)
        for first in range(0, wide, tokens):
            part = s_ref[first : first + tokens].reshape(tokens // 8, 8, CHUNK)
            peak = jnp.maximum(peak, jnp.max(part, axis=0))
        peak = jnp.max(peak, axis=0, keepdims=True)
        total = jnp.zeros((8, CHUNK), f32)
        for first in range(0, wide, tokens):
            p = jnp.exp2((s_ref[first : first + tokens] - peak) * factor)
            s_ref[first : first + tokens] = p
            total = total + jnp.sum(p.reshape(tokens // 8, 8, CHUNK), axis=0)
        inverse = 1.0 / jnp.sum(total, axis=0, keepdims=True)
        for first in range(0, wide, tokens):
            p = s_ref[first : first + tokens] * inverse
            wds_ref[first : first + tokens, :CHUNK] = p.astype(bf16)
            wds_ref[first : first + tokens, CHUNK:] = (
                p * dp_ref[first : first + tokens]
            ).astype(bf16)
        acc[spans[c]] += jnp.dot(wds_ref[...], zq_buf[c], preferred_element_type=f32)
        dq_buf[c] = lax.dot_general(
            k_buf[spans[c]], wds_ref[:, CHUNK:], tn, preferred_element_type=f32
        )

    grad_q = jnp.concatenate([jnp.transpose(dq_buf[c]) for c in range(chunks)], axis=0)
    grad_q = (SCALE * grad_q).astype(bf16)
    for row in range(REACH):
        last = GROUP + REACH + row
        to_above[0, row] = acc[row * tokens : (row + 1) * tokens].astype(bf16)
        to_below[0, row] = acc[last * tokens : (last + 1) * tokens].astype(bf16)
    for row in range(GROUP):
        own_ref[0, row] = acc[(REACH + row) * tokens : (REACH + row + 1) * tokens]
        dq = grad_q[row * tokens : (row + 1) * tokens]
        dq_ref[0, row] = jnp.where(low_half[:half], dq[:half], pltpu.roll(dq[half:], HEAD, 1))


def sum_kernel(me_ref, own_ref, above_ref, below_ref, dq_ref, *rest):
    outs, (pieces, sem) = rest[:GROUP], rest[GROUP:]
    tokens, half = own_ref.shape[2], dq_ref.shape[2]
    for head in range(own_ref.shape[0]):
        for row in range(GROUP):
            value = own_ref[head, row]
            if row < REACH:
                value = value + above_ref[head, row].astype(jnp.float32)
            if row >= GROUP - REACH:
                value = value + below_ref[head, row - GROUP + REACH].astype(jnp.float32)
            value = jnp.where(lanes_below(value.shape), value * SCALE, value)
            first = head * (tokens + half)
            pieces[row, first : first + tokens] = value.astype(jnp.bfloat16)
            pieces[row, first + tokens : first + tokens + half] = dq_ref[head, row]
    send_pieces(pieces, outs, sem, me_ref[0])


def unpack_kernel(split, me_ref, *refs):
    sets = len(split)
    parts, (q_out, k_out, v_out) = refs[: sets * GROUP], refs[sets * GROUP : sets * GROUP + 3]
    buffers = refs[sets * GROUP + 3 :]
    me = me_ref[0]
    tokens = k_out.shape[0]
    half = tokens // 2
    per = sum(split)
    for at in range(sets):
        for slot in range(GROUP):
            buffers[at][jnp.bitwise_xor(me, slot)] = parts[at * GROUP + slot][...]
    where = [(at, index) for at, number in enumerate(split) for index in range(number)]

    def piece(head):
        group, local = divmod(head, per)
        at, index = where[local]
        first = index * (tokens + half)
        return (
            buffers[at][group, first : first + tokens],
            buffers[at][group, first + tokens : first + tokens + half],
        )

    for pair in range(GROUP * per // 2):
        columns = slice(pair * LANES, (pair + 1) * LANES)
        (a, qa), (b, qb) = piece(2 * pair), piece(2 * pair + 1)
        below = lanes_below(qa.shape)
        q_out[:half, columns] = jnp.where(below, qa, pltpu.roll(qb, HEAD, 1))
        q_out[half:, columns] = jnp.where(below, pltpu.roll(qa, HEAD, 1), qb)
        below = lanes_below(a.shape)
        k_out[:, columns] = jnp.where(below, a, pltpu.roll(b, HEAD, 1))
        v_out[:, columns] = jnp.where(below, pltpu.roll(a, HEAD, 1), b)


def weight_part(count, at, o_ref, grad_ref, send_ref, left_ref, permuted):
    block = o_ref.shape[1] // count
    bits = count.bit_length() - 1
    order = [sum((i >> b & 1) << (bits - 1 - b) for b in range(bits)) for i in range(count)]
    for at_block, owner in enumerate(order):
        columns = slice(owner * block, (owner + 1) * block)
        permuted[:, at_block * block : (at_block + 1) * block] = o_ref[:, columns]
    rows = send_ref.shape[0]
    mine = at % 2
    send_ref[...] = outer(
        permuted[:, pl.ds(pl.multiple_of((1 - mine) * rows, rows), rows)], grad_ref[...]
    ).astype(send_ref.dtype)
    left_ref[...] = permuted[:, pl.ds(pl.multiple_of(mine * rows, rows), rows)]


def outer(left, right):
    return lax.dot_general(
        left, right, (((0,), (0,)), ((), ())), preferred_element_type=jnp.float32
    )


def second_kernel(at_ref, left_ref, grad_ref, received_ref, keep_ref, send_ref):
    rows = keep_ref.shape[0]
    mine = at_ref[0] // 2 % 2
    first, second = left_ref[:, :rows], left_ref[:, rows:]
    for other, out in ((1, send_ref), (0, keep_ref)):
        part = jnp.bitwise_xor(mine, other)
        place = pl.ds(pl.multiple_of(part * rows, rows), rows)
        left = jnp.where(part == 0, first, second)
        value = outer(left, grad_ref[...]) + received_ref[place].astype(jnp.float32)
        out[...] = value.astype(out.dtype)


def fold_kernel(bit, at_ref, kept_ref, received_ref, keep_ref, send_ref):
    rows = keep_ref.shape[0]
    mine = at_ref[0] // (1 << bit) % 2
    for other, out in ((1, send_ref), (0, keep_ref)):
        place = pl.ds(pl.multiple_of(jnp.bitwise_xor(mine, other) * rows, rows), rows)
        out[...] = (kept_ref[place] + received_ref[place].astype(jnp.float32)).astype(out.dtype)


def last_kernel(kept_ref, received_ref, out_ref):
    out_ref[...] = kept_ref[...] + received_ref[...].astype(jnp.float32)


def body(queries, keys, values, outputs, grad_out, w_out, bounds):
    own_rows, cols, tile, features = queries.shape
    tokens = own_rows * cols * tile
    half = tokens // 2
    heads = features // HEAD
    per = heads // GROUP
    count = lax.axis_size("row")
    assert own_rows == 1 and count % GROUP == 0 and heads % GROUP == 0
    bf16 = jnp.bfloat16
    position = lax.axis_index("row")
    me = (position % GROUP).astype(jnp.int32)
    first_row = position - me
    me_arr = me.reshape(1)
    q2, k2, v2, o2 = [x.reshape(tokens, features) for x in (queries, keys, values, outputs)]
    g2 = grad_out.reshape(tokens, -1)

    def exchange(pieces):
        result = [pieces[0]]
        for slot in range(1, GROUP):
            pairs = [(i, i ^ slot) for i in range(count)]
            result.append(near(lax.ppermute(pieces[slot], "row", pairs)))
        return result

    def shift(value, step):
        pairs = [(i, i + step) for i in range(count) if 0 <= i + step < count]
        return near(lax.ppermute(value, "row", pairs))

    def after(value, *others):
        return lax.optimization_barrier((value, *others))[0]

    piece = (per, tokens, LANES)
    kv = kernel_call(
        functools.partial(pack_kv_kernel, heads),
        out_shape=[jax.ShapeDtypeStruct(piece, bf16)] * GROUP,
        in_specs=[SMEM_SPEC, VMEM_SPEC, VMEM_SPEC],
        out_specs=[ANY_SPEC] * GROUP,
        scratch_shapes=[pltpu.VMEM((GROUP,) + piece, bf16), pltpu.SemaphoreType.DMA((GROUP,))],
        compiler_params=PARAMS,
        name="pack_kv",
            micros=MICROS["pack_kv"],
    )(me_arr, k2, v2)
    kv = exchange(kv)

    bits = count.bit_length() - 1
    halving = count == 1 << bits and features // count % 16 == 0
    shape = jax.ShapeDtypeStruct
    width = g2.shape[1]
    at_arr = position.astype(jnp.int32).reshape(1)

    def hop(sent, bit):
        return near(lax.ppermute(sent, "row", [(i, i ^ (1 << bit)) for i in range(count)]))

    def halves(kernel, rows, bit, operands):
        return kernel_call(
            kernel,
            out_shape=[shape((rows, width), jnp.float32), shape((rows, width), bf16)],
            in_specs=[SMEM_SPEC] + [VMEM_SPEC] * (len(operands) - 1),
            out_specs=[VMEM_SPEC] * 2,
            compiler_params=PARAMS,
            name="fold",
            micros=MICROS["fold"],
        )(*operands)

    def fold(bit, kept, sent, other):
        operands = (after(at_arr, other), kept, hop(sent, bit))
        return halves(functools.partial(fold_kernel, bit + 1), kept.shape[0] // 2, bit, operands)

    qd_rows = per * tokens + 16 * (-(-tokens // LANES))
    rows = features // 2
    made = kernel_call(
        functools.partial(pack_qd_kernel, heads, count if halving else 0),
        out_shape=[shape((qd_rows, LANES), bf16)] * GROUP
        + [shape((rows, width), bf16), shape((tokens, rows), bf16)] * halving,
        in_specs=[SMEM_SPEC] + [VMEM_SPEC] * 4,
        out_specs=[ANY_SPEC] * GROUP + [VMEM_SPEC] * (2 * halving),
        scratch_shapes=[
            pltpu.VMEM((GROUP, qd_rows, LANES), bf16),
            pltpu.SemaphoreType.DMA((GROUP,)),
            pltpu.VMEM((tokens, features), bf16),
        ]
        + [pltpu.VMEM((tokens, features), bf16)] * halving,
        compiler_params=PARAMS,
        name="pack_qd",
        micros=MICROS["pack_qd"],
    )(after(jnp.concatenate([me_arr, at_arr]), kv[1]), q2, g2, w_out, o2)
    qd = made[:GROUP]
    if halving:
        sent, left = made[GROUP:]
    qd_sent = qd[1]
    qd = exchange(qd)

    groups = [number for number in (per - 1, 1) if number]
    window = (REACH, tokens, LANES)
    borders = kernel_call(
        halo_kernel,
        out_shape=[shape((per,) + window, bf16)] * 2,
        in_specs=[SMEM_SPEC] + [VMEM_SPEC] * GROUP,
        out_specs=[VMEM_SPEC] * 2,
        compiler_params=PARAMS,
        name="halo",
        micros=MICROS["halo"],
    )(after(me_arr, qd_sent), *kv)

    if halving:
        kept, sent = halves(
            second_kernel, features // 4, 0, (after(at_arr, borders[0]), left, g2, hop(after(sent, borders[0]), 0))
        )
    folds = 1
    limits = lax.dynamic_slice_in_dim(bounds, first_row, GROUP, 0).reshape(-1)
    scalars = jnp.concatenate([me_arr, first_row.reshape(1), limits])
    rows_all = GROUP + 2 * REACH
    chunks = GROUP * tokens // CHUNK
    results = []
    head = 0
    above = shift(borders[0], GROUP)
    below = shift(borders[1], -GROUP)
    for number in groups:
        if halving:
            scalars = after(scalars, kept)
        here = lambda i: (i, 0, 0, 0)
        result = kernel_call(
            functools.partial(attention_kernel, per, cols, head),
            grid=(number,),
            out_shape=[
                shape((number,) + window, bf16),
                shape((number,) + window, bf16),
                shape((number, GROUP, tokens, LANES), jnp.float32),
                shape((number, GROUP, half, LANES), bf16),
            ],
            in_specs=[SMEM_SPEC] + [VMEM_SPEC] * (2 * GROUP + 2),
            out_specs=[
                pl.BlockSpec((1,) + window, here),
                pl.BlockSpec((1,) + window, here),
                pl.BlockSpec((1, GROUP, tokens, LANES), here),
                pl.BlockSpec((1, GROUP, half, LANES), here),
            ],
            scratch_shapes=[pltpu.VMEM((rows_all * tokens, LANES), bf16)] * 2
            + [pltpu.VMEM((GROUP * tokens, LANES), bf16)] * 2
            + [
                pltpu.VMEM((2, WINDOW * tokens, CHUNK), jnp.float32),
                pltpu.VMEM((2, WINDOW * tokens, CHUNK), jnp.float32),
                pltpu.VMEM((2, WINDOW * tokens, 2 * CHUNK), bf16),
                pltpu.VMEM((chunks, 2 * CHUNK, LANES), bf16),
                pltpu.VMEM((rows_all * tokens, LANES), jnp.float32),
                pltpu.VMEM((chunks, LANES, CHUNK), jnp.float32),
            ],
            compiler_params=PARAMS,
            name="attention",
            micros=MICROS["attention"] * number,
        )(scalars, *kv, above, below, *qd)
        results.append(result)
        head += number
        if halving and folds < bits - 1:
            kept, sent = fold(folds, kept, sent, result[2])
            folds += 1

    returned = []
    turn = after(me_arr, results[-1][2])
    for number, (to_above, to_below, own, dq) in zip(groups, results):
        size = (number * (tokens + half), LANES)
        pieces = kernel_call(
            sum_kernel,
            out_shape=[shape(size, bf16)] * GROUP,
            in_specs=[SMEM_SPEC] + [VMEM_SPEC] * 4,
            out_specs=[ANY_SPEC] * GROUP,
            scratch_shapes=[pltpu.VMEM((GROUP,) + size, bf16), pltpu.SemaphoreType.DMA((GROUP,))],
            compiler_params=PARAMS,
            name="sum",
            micros=MICROS["sum"],
        )(turn, own, shift(to_below, GROUP), shift(to_above, -GROUP), dq)
        returned += exchange(pieces)
        while halving and folds < bits - 1:
            kept, sent = fold(folds, kept, sent, pieces[0])
            folds += 1
        turn = after(me_arr, returned[3], *([kept] if halving else []))

    if halving:
        grad_w_out = kernel_call(
            last_kernel,
            out_shape=shape(kept.shape, jnp.float32),
            in_specs=[VMEM_SPEC] * 2,
            out_specs=VMEM_SPEC,
            name="last",
            micros=MICROS["last"],
        )(kept, hop(sent, bits - 1))
    else:
        grad_w_out = lax.psum_scatter(
            lax.dot_general(o2, g2, (((0,), (0,)), ((), ())), preferred_element_type=jnp.float32),
            "row",
            scatter_dimension=0,
            tiled=True,
        )

    grads = kernel_call(
        functools.partial(unpack_kernel, groups),
        out_shape=[shape((tokens, features), bf16)] * 3,
        in_specs=[SMEM_SPEC] + [VMEM_SPEC] * (len(groups) * GROUP),
        out_specs=[VMEM_SPEC] * 3,
        scratch_shapes=[
            pltpu.VMEM((GROUP, number * (tokens + half), LANES), bf16) for number in groups
        ],
        compiler_params=PARAMS,
        name="unpack",
            micros=MICROS["unpack"],
    )(me_arr, *[near(x) for x in returned])
    grads = [x.reshape(queries.shape) for x in grads]
    return (*grads, grad_w_out)


def solution(mesh):
    placed = P(("groups", "row"), None, None, None)
    return jax.shard_map(
        body,
        mesh=mesh,
        in_specs=(placed, placed, placed, placed, placed, P(), P("groups", None)),
        out_specs=(placed, placed, placed, P(("groups", "row"), None)),
        check_vma=False,
    )
```
